32 devices in a mesh: gx: 8 (over z, y), gy: 4 (over x, core).
Axes of the slice: x: 2, y: 2, z: 4, core: 2. Of those that a mesh axis runs over, the one named last changes fastest.
Arguments:
- magnet: float32 [3, 32, 2048], P(None, 'gx', 'gy'), may hold values from -1 to 1, as said below
- thermal: float32 [3, 3, 32, 2048], P(None, None, 'gx', 'gy'), may hold values from -4 to 4
- kernel_diag: float32 [3, 128, 64, 64], P(None, 'gy', 'gx'), may hold values from 0.05 to 0.6, as said below
- kernel_off: float32 [3, 128, 64, 64], P(None, 'gy', 'gx'), may hold values from -0.25 to 0.25, as said below
Outputs:
- final_magnet: float32 [3, 32, 2048], P(None, 'gx', 'gy')
- demag_field: float32 [3, 32, 2048], P(None, 'gx', 'gy')
The draws below stay inside these ranges and needn't reach their ends.
Inputs may be any that keep to these rules, and one draw needn't show every extreme that they name: `magnet`: each cell's three components form a unit vector. `kernel_diag`: each entry at (kz, ky, kx) equals the entry at (-kz, -ky, -kx), indices taken modulo 2 * 64, 64, 64. `kernel_off`: each entry at (kz, ky, kx) equals the entry at (-kz, -ky, -kx), indices taken modulo 2 * 64, 64, 64.
All inputs are finite; a program needn't handle non-finite values.
Results may differ from the reference program's by a relative error of at most 0.0001.
Values sent between devices are 32-bit elements; how exact they have to be, the bound alone decides.
A program may use at most 64 MiB of HBM per device.

```python
import math
import jax
import jax.numpy as jnp
from jax import lax

NZ = 64
STEPS = 3
NX = 32
NY = 32


def draw_magnet(key, part):
    first_key, second_key = jax.random.split(key)
    shape = (NX, NY * NZ)
    polar = jax.random.uniform(first_key, shape, jnp.float32, -1.0, 1.0)
    azimuth = jax.random.uniform(second_key, shape, jnp.float32, -math.pi, math.pi)
    radial = jnp.sqrt(jnp.maximum(1.0 - polar * polar, 0.0))
    return jnp.stack([radial * jnp.cos(azimuth), radial * jnp.sin(azimuth), polar]).astype(jnp.float32)


def even_field(key, lower, upper):
    shape = (3, 2 * NZ, 2 * NY, 2 * NX)
    values = jax.random.uniform(key, shape, jnp.float32, lower, upper)
    mirrored = jnp.roll(jnp.flip(values, (1, 2, 3)), 1, (1, 2, 3))
    return (0.5 * (values + mirrored)).astype(jnp.float32)


def draw_kernel_diag(key, part):
    return even_field(jax.random.fold_in(key, 11), 0.05, 0.6)


def draw_kernel_off(key, part):
    return even_field(jax.random.fold_in(key, 23), -0.25, 0.25)


def block_scale(own_key, shape, cuts, smallest, top_value):
    loudness, own = 1.0, jax.random.fold_in(own_key, 6)
    for position, shards_of in cuts:
        heights = jnp.exp(jax.random.uniform(jax.random.fold_in(own, position), (shards_of,), jnp.float32, smallest / len(cuts), top_value / len(cuts)))
        loudness = loudness * jnp.repeat(heights, shape[position] // shards_of).reshape([-1 if axis == position else 1 for axis in range(len(shape))])
    return loudness


def bell_draw(own_key, shape, deviation, limit, shards=(), kind=jnp.bfloat16):
    factor_of = block_scale(own_key, shape, shards, -0.22, 0.18) if shards else 1.0
    drawn = jax.random.normal(own_key, shape, jnp.float32) * deviation * factor_of
    return jnp.minimum(jnp.maximum(drawn, -limit), limit).astype(kind)


def setup_inputs(seed: int = 0) -> dict:
    seeds = jax.random.split(jax.random.key(seed), 5)
    return {
        "magnet": draw_magnet(jax.random.fold_in(seeds[4], 71), 0),
        "thermal": bell_draw(seeds[1], (STEPS, 3, NX, NY * NZ), 1.0, 4.0, ((2, 8), (3, 4)), jnp.float32),
        "kernel_diag": draw_kernel_diag(jax.random.fold_in(seeds[4], 71), 0),
        "kernel_off": draw_kernel_off(jax.random.fold_in(seeds[4], 71), 0),
    }


damping = 0.1
time_step = 0.05
anisotropy = 0.5

def cross(left, right):
    return jnp.stack([left[1] * right[2] - left[2] * right[1], left[2] * right[0] - left[0] * right[2], left[0] * right[1] - left[1] * right[0]])

def torque(field, heff):
    first = cross(field, heff)
    return -(first + damping * cross(field, first)) / (1.0 + damping * damping)

def laplace(field):
    padded = jnp.pad(field, ((0, 0), (1, 1), (1, 1), (1, 1)), mode='edge')
    center = padded[:, 1:-1, 1:-1, 1:-1]
    total = padded[:, 2:, 1:-1, 1:-1] + padded[:, :-2, 1:-1, 1:-1]
    total = total + padded[:, 1:-1, 2:, 1:-1] + padded[:, 1:-1, :-2, 1:-1]
    total = total + padded[:, 1:-1, 1:-1, 2:] + padded[:, 1:-1, 1:-1, :-2]
    return total - 6.0 * center

def effective(field, demag, noise):
    heff = laplace(field) + demag + noise
    return heff.at[2].add(anisotropy * field[2])

def demagnetize(field, kernel_diag, kernel_off):
    padded = jnp.pad(field, ((0, 0), (0, NX), (0, NY), (0, NZ)))
    spectra = jnp.fft.fftn(padded, axes=(1, 2, 3))
    diag = jnp.transpose(kernel_diag, (0, 3, 2, 1))
    off = jnp.transpose(kernel_off, (0, 3, 2, 1))
    hx = diag[0] * spectra[0] + off[0] * spectra[1] + off[1] * spectra[2]
    hy = off[0] * spectra[0] + diag[1] * spectra[1] + off[2] * spectra[2]
    hz = off[1] * spectra[0] + off[2] * spectra[1] + diag[2] * spectra[2]
    result = []
    for comp in (hx, hy, hz):
        back = jnp.fft.ifftn(comp)
        result.append(-jnp.real(back)[:NX, :NY, :NZ])
    return jnp.stack(result).astype(jnp.float32)

def reference(magnet, thermal, kernel_diag, kernel_off):
    field = magnet.reshape(3, NX, NY, NZ)
    demag = demagnetize(field, kernel_diag, kernel_off)
    for step in range(STEPS):
        noise = thermal[step].reshape(3, NX, NY, NZ)
        first = torque(field, effective(field, demag, noise))
        trial = field + time_step * first
        second = torque(trial, effective(trial, demag, noise))
        update = field + 0.5 * time_step * (first + second)
        field = update / jnp.sqrt(lax.optimization_barrier(jnp.sum(update * update, axis=0, keepdims=True)))
    return (field.reshape(3, NX, NY * NZ), demag.reshape(3, NX, NY * NZ))
```

```python
import functools

import jax
import jax.numpy as jnp
import ml_dtypes
import numpy as np
from jax import lax
from jax.experimental import pallas as pl
from jax.experimental.pallas import tpu as pltpu
from jax.sharding import PartitionSpec as P

NZ = 64
STEPS = 3
DAMPING = 0.1
TIME_STEP = 0.05
ANISOTROPY = 0.5
LX = 4
LY = 8
MESH = pl.DeviceIdType.MESH
OFFSETS = [(dx, dy) for dx in (-2, -1, 0, 1, 2) for dy in (-1, 0, 1) if (dx, dy) != (0, 0)]
PLACE = {-2: (0, 1, 1), -1: (1, 0, 2), 0: (3, 0, 2), 1: (5, 0, 2), 2: (7, 0, 1)}


def halves(table):
    table = np.asarray(table, np.float32)
    high = table.astype(ml_dtypes.bfloat16)
    low = (table - high.astype(np.float32)).astype(ml_dtypes.bfloat16)
    return np.stack([high, low])


def angles(first, second, period):
    return 2.0 * np.pi * ((np.asarray(first)[:, None] * np.asarray(second)[None, :]) % period) / period


def tables(nx, ny):
    x_all, y_all = nx * LX, ny * LY
    block = 2 * NZ // ny
    kept = block // 2 + 1
    ang = angles(np.arange(2 * y_all), np.arange(y_all), 2 * y_all)
    y_fwd = np.concatenate([np.cos(ang), -np.sin(ang)])
    z_fwd = np.zeros((ny, 3, 2, NZ, 128))
    z_inv = np.zeros((ny, 128, 3, 2, NZ))
    for g in range(ny):
        kz = g * block + np.arange(kept)
        ang = angles(np.arange(NZ), kz, 2 * NZ)
        weight = np.full((kept,), 2.0)
        if g in (0, ny // 2):
            weight[0] = 1.0
        if g > ny // 2:
            weight[0] = 0.0
        if g < ny // 2:
            weight[kept - 1] = 0.0
        weight = -weight / (8.0 * x_all * y_all * NZ)
        for c in range(3):
            re = slice(c * kept, (c + 1) * kept)
            im = slice(64 + c * kept, 64 + (c + 1) * kept)
            z_fwd[g, c, 0, :, re] = np.cos(ang)
            z_fwd[g, c, 1, :, re] = np.sin(ang)
            z_fwd[g, c, 1, :, im] = np.cos(ang)
            z_fwd[g, c, 0, :, im] = -np.sin(ang)
            for copy in range(2):
                z_inv[g, re, c, copy] = (np.cos(ang) * weight).T
                z_inv[g, im, c, copy] = (-np.sin(ang) * weight).T
    z_fwd = z_fwd.reshape(ny, 3 * 2 * NZ, 128)
    z_inv = z_inv.reshape(ny * 128, 3 * 128)
    ang = angles(np.arange(2 * x_all), np.arange(x_all), 2 * x_all)
    eye = np.eye(8)
    x_fwd = np.stack([np.cos(ang), np.sin(ang)])
    x_inv = np.einsum("skx,ab->sxabk", x_fwd, eye).reshape(2 * x_all * 8, 8 * 2 * x_all)
    x_fwd = np.einsum("skx,ab->sakxb", x_fwd, eye).reshape(2 * 8 * 2 * x_all, x_all * 8)
    ang = angles(np.arange(y_all), np.arange(2 * y_all), 2 * y_all)
    y_inv = np.concatenate([np.cos(ang), np.sin(ang)])
    place = np.zeros((3, 2, 3, block, 128))
    pairs = {(0, 1): 0, (0, 2): 1, (1, 2): 2}
    for c in range(3):
        for d in range(3):
            other = (c + d) % 3
            entry = c if d == 0 else pairs[(min(c, other), max(c, other))]
            for half in range(2):
                for j in range(kept):
                    place[d, :, entry, j, half * 64 + c * kept + j] = 1.0
    place = place.reshape(3, 6 * block, 128)
    place = np.concatenate([place[0], place[1], place[2]], axis=1).astype(ml_dtypes.bfloat16)
    return (
        halves(y_fwd),
        np.moveaxis(halves(z_fwd), 0, 1),
        halves(x_fwd),
        halves(x_inv),
        halves(y_inv),
        halves(z_inv),
        place,
    )


def split(value):
    high = value.astype(jnp.bfloat16)
    low = (value - high.astype(jnp.float32)).astype(jnp.bfloat16)
    return high, low


def dot(left, right):
    return jnp.dot(left, right, preferred_element_type=jnp.float32)


def dot_left(table, data):
    high, low = split(data)
    return dot(table[0], high) + (dot(table[0], low) + dot(table[1], high))


def dot_right(data, table):
    high, low = split(data)
    return dot(high, table[0]) + (dot(low, table[0]) + dot(high, table[1]))


def cross(a, b):
    return [a[1] * b[2] - a[2] * b[1], a[2] * b[0] - a[0] * b[2], a[0] * b[1] - a[1] * b[0]]


def kernel(
    nx, ny,
    fields, diag_h, off_h, y_fwd_h, z_fwd_h, x_fwd_h, x_inv_h, y_inv_h, z_inv_h, place_h,
    final_ref, demag_ref,
    diag, off, y_fwd, z_small, z_fwd, x_fwd, x_inv, y_inv, z_inv, place,
    wide, wide_demag, rows_in, spec_out, spec_in, back_out, back_in, row_out, row_in, tensor,
    local_sem, halo_send, halo_recv, dem_send, dem_recv, ag_send, ag_recv,
    fwd_send, fwd_recv, inv_send, inv_recv, last_send, last_recv,
):
    x_all, y_all = nx * LX, ny * LY
    block = 2 * NZ // ny
    kept = block // 2 + 1
    me_x, me_y = lax.axis_index("gx"), lax.axis_index("gy")

    loads = [
        pltpu.make_async_copy(src, dst, local_sem.at[i])
        for i, (src, dst) in enumerate([
            (y_fwd_h, y_fwd), (z_fwd_h.at[me_y], z_small), (diag_h, diag), (off_h, off),
            (place_h, place), (x_fwd_h, x_fwd), (x_inv_h, x_inv), (y_inv_h, y_inv), (z_inv_h, z_inv),
        ])
    ]
    for load in loads:
        load.start()

    def present(dx, dy):
        x, y = me_x + dx, me_y + dy
        return (x >= 0) & (x < nx) & (y >= 0) & (y < ny)

    barrier = pltpu.get_barrier_semaphore()
    diagonal = [(dx, dy) for dx, dy in OFFSETS if dx and dy]
    for i in range(1, nx):
        pl.semaphore_signal(barrier, 1, device_id=(lax.rem(me_x + i, nx), me_y), device_id_type=MESH)
    for i in range(1, ny):
        pl.semaphore_signal(barrier, 1, device_id=(me_x, lax.rem(me_y + i, ny)), device_id_type=MESH)
    for dx, dy in diagonal:
        @pl.when(present(dx, dy))
        def _():
            pl.semaphore_signal(barrier, 1, device_id=(me_x + dx, me_y + dy), device_id_type=MESH)
    beside_x = jnp.minimum(me_x, 2) + jnp.minimum(nx - 1 - me_x, 2)
    beside_y = jnp.minimum(me_y, 1) + jnp.minimum(ny - 1 - me_y, 1)
    pl.semaphore_wait(barrier, nx + ny - 2 + beside_x * beside_y)

    def along_y(i, src, dst, send, recv):
        return pltpu.make_async_remote_copy(
            src, dst, send.at[i], recv.at[i],
            device_id=(me_x, lax.rem(me_y + i, ny)), device_id_type=MESH)

    def along_x(i, src, dst, send, recv):
        return pltpu.make_async_remote_copy(
            src, dst, send.at[i], recv.at[i],
            device_id=(lax.rem(me_x + i, nx), me_y), device_id_type=MESH)

    gather = [along_y(i, fields.at[0], rows_in.at[me_y], ag_send, ag_recv) for i in range(1, ny)]
    for copy in gather:
        copy.start()

    def halo(i, kind):
        dx, dy = OFFSETS[i]
        at, first, count = PLACE[-dx]
        if kind == 0:
            many = 2 if abs(dx) == 2 else 4
            src = fields.at[pl.ds(0, many), :, pl.ds(first, count)]
            dst = wide.at[pl.ds(0, many), :, pl.ds(at, count), 1 - dy]
            send, recv = halo_send, halo_recv
        else:
            src = demag_ref.at[:, pl.ds(first, count)]
            dst = wide_demag.at[:, pl.ds(at, count), 1 - dy]
            send, recv = dem_send, dem_recv
        return pltpu.make_async_remote_copy(
            src, dst, send.at[i], recv.at[i],
            device_id=(me_x + dx, me_y + dy), device_id_type=MESH)

    def halo_start(kind):
        for i, (dx, dy) in enumerate(OFFSETS):
            @pl.when(present(dx, dy))
            def _():
                halo(i, kind).start()

    def halo_wait(kind):
        for i, (dx, dy) in enumerate(OFFSETS):
            @pl.when(present(dx, dy))
            def _():
                halo(i, kind).wait_send()

            @pl.when(present(-dx, -dy))
            def _():
                halo(i, kind).wait_recv()

    halo_start(0)
    wide[0:4, :, 3:5, 1] = fields[...]
    rows_in[me_y] = fields[0]

    for i in (2, 3, 4):
        loads[i].wait()
    for y in range(8):
        for source, first, last in ((diag, 0, 128), (off, 128, 384)):
            piece = source[:, :, y, :].reshape(3 * block, 2 * x_all)
            high, low = split(piece)
            both = jnp.concatenate([high, low], axis=0)
            tensor[pl.ds(y * 2 * x_all, 2 * x_all), first:last] = lax.dot_general(
                both, place[:, first:last], (((0,), (0,)), ((), ())), preferred_element_type=jnp.float32)

    loads[1].wait()
    z_fwd[...] = jnp.zeros_like(z_fwd)
    for x in range(2):
        for part in range(6):
            z_fwd[:, pl.ds(128 * part + NZ * x, NZ), 128 * x : 128 * (x + 1)] = z_small[:, pl.ds(NZ * part, NZ)]
    loads[0].wait()
    for copy in gather:
        copy.wait()
    data = jnp.concatenate(
        [rows_in[:, c, t].reshape(y_all, 128) for c in range(3) for t in range(2)], axis=1)
    spectrum = dot_left(y_fwd, data)
    for t in range(2):
        parts = []
        for c in range(3):
            lanes = slice((2 * c + t) * 128, (2 * c + t + 1) * 128)
            parts += [spectrum[: 2 * y_all, lanes], spectrum[2 * y_all :, lanes]]
        planes = dot_right(jnp.concatenate(parts, axis=1), z_fwd)
        for x in range(2):
            spec_out[:, 2 * t + x] = planes[:, x * 128 : (x + 1) * 128].reshape(nx, 8, 128)
    forward = [
        along_x(i, spec_out.at[lax.rem(me_x + i, nx)], spec_in.at[me_x], fwd_send, fwd_recv)
        for i in range(1, nx)
    ]
    for copy in forward:
        copy.start()
    spec_in[me_x] = spec_out[me_x]
    loads[5].wait()
    loads[6].wait()
    lane = lax.broadcasted_iota(jnp.int32, (1, 128), 1)
    low_half = lane < 64
    component = lax.rem(lane, 64)
    turn = jnp.where(low_half, 1.0, -1.0).astype(jnp.float32)
    for copy in forward:
        copy.wait()

    size = 8 * 2 * x_all
    both = dot_left(x_fwd, spec_in[...].reshape(x_all * 8, 128))
    spectra = both[:size] + turn * pltpu.roll(both[size:], 64, 1)
    second = jnp.where(component < 2 * kept, pltpu.roll(spectra, 128 - kept, 1), pltpu.roll(spectra, 2 * kept, 1))
    third = jnp.where(component < kept, pltpu.roll(spectra, 128 - 2 * kept, 1), pltpu.roll(spectra, kept, 1))
    response = tensor[:, :128] * spectra + tensor[:, 128:256] * second + tensor[:, 256:] * third
    both = dot_left(x_inv, response)
    back = both[: x_all * 8] - turn * pltpu.roll(both[x_all * 8 :], 64, 1)
    back_out[...] = back.reshape(nx, LX, 8, 128)
    inverse = [
        along_x(i, back_out.at[lax.rem(me_x + i, nx)], back_in.at[me_x], inv_send, inv_recv)
        for i in range(1, nx)
    ]
    for copy in inverse:
        copy.start()
    back_in[me_x] = back_out[me_x]
    loads[7].wait()
    loads[8].wait()
    for copy in inverse:
        copy.wait()
    data = jnp.concatenate([back_in[:, x].reshape(nx * 8, 128) for x in range(LX)], axis=1)
    both = dot_left(y_inv, data)
    for x in range(LX):
        lanes = slice(x * 128, (x + 1) * 128)
        rows = both[:y_all, lanes] - turn * pltpu.roll(both[y_all:, lanes], 64, 1)
        row_out[:, x] = rows.reshape(ny, LY, 128)
    final = [
        along_y(i, row_out.at[lax.rem(me_y + i, ny)], row_in.at[me_y], last_send, last_recv)
        for i in range(1, ny)
    ]
    for copy in final:
        copy.start()
    row_in[me_y] = row_out[me_y]
    for copy in final:
        copy.wait()
    data = jnp.concatenate([row_in[g].reshape(LX * LY, 128) for g in range(ny)], axis=1)
    rows = dot_right(data, z_inv)
    for c in range(3):
        lanes = slice(c * 128, (c + 1) * 128)
        for t in range(2):
            demag_ref[c, t] = jnp.where(
                low_half, rows[16 * t : 16 * t + 8, lanes], rows[16 * t + 8 : 16 * t + 16, lanes])
    halo_start(1)
    wide_demag[:, 3:5, 1] = demag_ref[...]
    halo_wait(0)
    halo_wait(1)

    shape = (8, 3 * LY, 128)
    lanes = lax.broadcasted_iota(jnp.int32, shape, 2)
    x_at = LX * me_x - 6 + 2 * lax.broadcasted_iota(jnp.int32, shape, 0) + lanes // 64
    y_at = LY * me_y - LY + lax.broadcasted_iota(jnp.int32, shape, 1)
    z_at = lax.rem(lanes, 64)
    left_half = lanes < 64
    at_x0, at_x1 = x_at == 0, x_at == x_all - 1
    at_y0, at_y1 = y_at == 0, y_at == y_all - 1
    at_z0, at_z1 = z_at == 0, z_at == NZ - 1

    def laplace(v):
        turned = pltpu.roll(v, 64, 2)
        up = jnp.where(left_half, turned, jnp.concatenate([turned[1:], turned[-1:]], axis=0))
        down = jnp.where(left_half, jnp.concatenate([turned[:1], turned[:-1]], axis=0), turned)
        total = jnp.where(at_x1, v, up) + jnp.where(at_x0, v, down)
        total = total + jnp.where(at_y1, v, pltpu.roll(v, 3 * LY - 1, 1))
        total = total + jnp.where(at_y0, v, pltpu.roll(v, 1, 1))
        total = total + jnp.where(at_z1, v, pltpu.roll(v, 127, 2))
        total = total + jnp.where(at_z0, v, pltpu.roll(v, 1, 2))
        return total - 6.0 * v

    def torque(v, noise):
        h = [laplace(v[c]) + noise[c] for c in range(3)]
        h[2] = h[2] + ANISOTROPY * v[2]
        first = cross(v, h)
        second = cross(v, first)
        return [(first[c] + DAMPING * second[c]) * (-1.0 / (1.0 + DAMPING * DAMPING)) for c in range(3)]

    m = [wide[0, c].reshape(shape) for c in range(3)]
    for s in range(STEPS):
        noise = [wide_demag[c].reshape(shape) + wide[1 + s, c].reshape(shape) for c in range(3)]
        f0 = torque(m, noise)
        f1 = torque([m[c] + TIME_STEP * f0[c] for c in range(3)], noise)
        u = [m[c] + 0.5 * TIME_STEP * (f0[c] + f1[c]) for c in range(3)]
        norm = jnp.sqrt(u[0] * u[0] + u[1] * u[1] + u[2] * u[2])
        m = [u[c] / norm for c in range(3)]
    for c in range(3):
        final_ref[c] = m[c][3:5, LY : 2 * LY]


def body(nx, ny, magnet, thermal, kernel_diag, kernel_off):
    block = 2 * NZ // ny
    x_all, y_all = nx * LX, ny * LY
    consts = tables(nx, ny)
    fields = jnp.concatenate([magnet[None], thermal])
    fields = fields.reshape(1 + STEPS, 3, LX // 2, 2, LY, NZ)
    fields = jnp.swapaxes(fields, 3, 4).reshape(1 + STEPS, 3, LX // 2, LY, 2 * NZ)
    vmem = pl.BlockSpec(memory_space=pltpu.VMEM)
    anyspace = pl.BlockSpec(memory_space=pl.ANY)
    out = jax.ShapeDtypeStruct((3, LX // 2, LY, 2 * NZ), jnp.float32)
    f32, bf16 = jnp.float32, jnp.bfloat16
    scratch = [
        pltpu.VMEM(kernel_diag.shape, f32),
        pltpu.VMEM(kernel_off.shape, f32),
        pltpu.VMEM(consts[0].shape, bf16),
        pltpu.VMEM(consts[1].shape[1:], bf16),
        pltpu.VMEM((2, 3 * 2 * 2 * NZ, 256), bf16),
        *[pltpu.VMEM(c.shape, bf16) for c in consts[2:]],
        pltpu.VMEM((1 + STEPS, 3, 8, 3, LY, 128), f32),
        pltpu.VMEM((3, 8, 3, LY, 128), f32),
        pltpu.VMEM((ny, 3, 2, LY, 128), f32),
        *[pltpu.VMEM((nx, LX, 8, 128), f32)] * 4,
        *[pltpu.VMEM((ny, LX, LY, 128), f32)] * 2,
        pltpu.VMEM((8 * 2 * x_all, 384), f32),
        pltpu.SemaphoreType.DMA((9,)),
        *[pltpu.SemaphoreType.DMA((len(OFFSETS),))] * 4,
        *[pltpu.SemaphoreType.DMA((ny,))] * 2,
        *[pltpu.SemaphoreType.DMA((nx,))] * 4,
        *[pltpu.SemaphoreType.DMA((ny,))] * 2,
    ]
    final, demag = pl.pallas_call(
        functools.partial(kernel, nx, ny),
        out_shape=(out, out),
        in_specs=[vmem] + [anyspace] * 9,
        out_specs=(vmem, vmem),
        scratch_shapes=scratch,
        compiler_params=pltpu.CompilerParams(
            collective_id=0, has_side_effects=True, vmem_limit_bytes=56 * 1024 * 1024),
    )(fields, kernel_diag, kernel_off, *[jnp.asarray(c) for c in consts])

    def natural(value):
        value = value.reshape(3, LX // 2, LY, 2, NZ)
        return jnp.swapaxes(value, 2, 3).reshape(3, LX, LY * NZ)

    return natural(final), natural(demag)


def solution(mesh):
    in_specs = (
        P(None, "gx", "gy"),
        P(None, None, "gx", "gy"),
        P(None, "gy", "gx", None),
        P(None, "gy", "gx", None),
    )
    out_specs = (P(None, "gx", "gy"), P(None, "gx", "gy"))
    run = functools.partial(body, mesh.shape["gx"], mesh.shape["gy"])
    return jax.shard_map(run, mesh=mesh, in_specs=in_specs, out_specs=out_specs, check_vma=False)
```

```python
import functools

import jax
import jax.numpy as jnp
import ml_dtypes
import numpy as np
from jax import lax
from jax.experimental import pallas as pl
from jax.experimental.pallas import tpu as pltpu
from jax.sharding import PartitionSpec as P

NZ = 64
STEPS = 3
DAMPING = 0.1
TIME_STEP = 0.05
ANISOTROPY = 0.5
LX = 4
LY = 8
MESH = pl.DeviceIdType.MESH
OFFSETS = [(dx, dy) for dx in (-2, -1, 0, 1, 2) for dy in (-1, 0, 1) if (dx, dy) != (0, 0)]
PLACE = {-2: (0, 1, 1), -1: (1, 0, 2), 0: (3, 0, 2), 1: (5, 0, 2), 2: (7, 0, 1)}


def halves(table):
    table = np.asarray(table, np.float32)
    high = table.astype(ml_dtypes.bfloat16)
    low = (table - high.astype(np.float32)).astype(ml_dtypes.bfloat16)
    return np.stack([high, low])


def angles(first, second, period):
    return 2.0 * np.pi * ((np.asarray(first)[:, None] * np.asarray(second)[None, :]) % period) / period


def tables(nx, ny):
    x_all, y_all = nx * LX, ny * LY
    block = 2 * NZ // ny
    kept = block // 2 + 1
    ang = angles(np.arange(2 * y_all), np.arange(y_all), 2 * y_all)
    y_fwd = np.concatenate([np.cos(ang), -np.sin(ang)])
    z_fwd = np.zeros((ny, 3, 2, NZ, 128))
    z_inv = np.zeros((ny, 128, 4, NZ))
    for g in range(ny):
        kz = g * block + np.arange(kept)
        ang = angles(np.arange(NZ), kz, 2 * NZ)
        weight = np.full((kept,), 2.0)
        if g in (0, ny // 2):
            weight[0] = 1.0
        if g > ny // 2:
            weight[0] = 0.0
        if g < ny // 2:
            weight[kept - 1] = 0.0
        weight = -weight / (8.0 * x_all * y_all * NZ)
        for c in range(3):
            re = slice(c * kept, (c + 1) * kept)
            im = slice(64 + c * kept, 64 + (c + 1) * kept)
            z_fwd[g, c, 0, :, re] = np.cos(ang)
            z_fwd[g, c, 1, :, re] = np.sin(ang)
            z_fwd[g, c, 1, :, im] = np.cos(ang)
            z_fwd[g, c, 0, :, im] = -np.sin(ang)
            z_inv[g, re, c] = (np.cos(ang) * weight).T
            z_inv[g, im, c] = (-np.sin(ang) * weight).T
    z_fwd = z_fwd.reshape(ny, 3 * 2 * NZ, 128)
    z_inv = z_inv.reshape(ny * 128, 4 * NZ)
    ang = angles(np.arange(2 * x_all), np.arange(x_all), 2 * x_all)
    eye = np.eye(8)
    x_fwd = np.stack([np.cos(ang), np.sin(ang)])
    x_inv = np.einsum("skx,ab->sxabk", x_fwd, eye).reshape(2 * x_all * 8, 8 * 2 * x_all)
    x_fwd = np.repeat(x_fwd.reshape(2 * 2 * x_all, x_all), 8, axis=1)
    ang = angles(np.arange(y_all), np.arange(2 * y_all), 2 * y_all)
    y_inv = np.concatenate([np.cos(ang), np.sin(ang)])
    place = np.zeros((3, 2, 3, block, 128))
    pairs = {(0, 1): 0, (0, 2): 1, (1, 2): 2}
    for c in range(3):
        for d in range(3):
            other = (c + d) % 3
            entry = c if d == 0 else pairs[(min(c, other), max(c, other))]
            for half in range(2):
                for j in range(kept):
                    place[d, :, entry, j, half * 64 + c * kept + j] = 1.0
    place = place.reshape(3, 6 * block, 128)
    place = np.concatenate([place[0], place[1], place[2]], axis=1).astype(ml_dtypes.bfloat16)
    return (
        halves(y_fwd),
        np.moveaxis(halves(z_fwd), 0, 1),
        halves(x_fwd),
        halves(x_inv),
        halves(y_inv),
        halves(z_inv),
        place,
    )


def split(value):
    high = value.astype(jnp.bfloat16)
    low = (value - high.astype(jnp.float32)).astype(jnp.bfloat16)
    return high, low


def dot(left, right):
    return jnp.dot(left, right, preferred_element_type=jnp.float32)


def dot_left(table, data):
    high, low = split(data)
    return dot(table[0], high) + (dot(table[0], low) + dot(table[1], high))


def dot_right(data, table):
    high, low = split(data)
    return dot(high, table[0]) + (dot(low, table[0]) + dot(high, table[1]))


def cross(a, b):
    return [a[1] * b[2] - a[2] * b[1], a[2] * b[0] - a[0] * b[2], a[0] * b[1] - a[1] * b[0]]


def kernel(
    nx, ny,
    magnet, thermal, diag_h, off_h, y_fwd_h, z_fwd_h, x_fwd_h, x_inv_h, y_inv_h, z_inv_h, place_h,
    final_ref, demag_ref,
    fields, demag, diag, off, y_fwd, z_small, z_fwd, x_small, x_fwd, x_inv, y_inv, z_inv, place,
    wide, wide_demag, rows_in, spec_out, spec_in, back_out, back_in, row_out, row_in, tensor,
    local_sem, side_send, side_recv, dem_send, dem_recv, ag_send, ag_recv,
    fwd_send, fwd_recv, inv_send, inv_recv, last_send, last_recv,
):
    x_all, y_all = nx * LX, ny * LY
    block = 2 * NZ // ny
    kept = block // 2 + 1
    me_x, me_y = lax.axis_index("gx"), lax.axis_index("gy")

    loads = [
        pltpu.make_async_copy(src, dst, local_sem.at[i])
        for i, (src, dst) in enumerate([
            (y_fwd_h, y_fwd), (z_fwd_h.at[me_y], z_small), (diag_h, diag), (off_h, off),
            (place_h, place), (x_fwd_h, x_small), (x_inv_h, x_inv), (y_inv_h, y_inv), (z_inv_h, z_inv),
        ])
    ]
    for load in loads:
        load.start()

    def present(dx, dy):
        x, y = me_x + dx, me_y + dy
        return (x >= 0) & (x < nx) & (y >= 0) & (y < ny)

    lane = lax.broadcasted_iota(jnp.int32, (1, 128), 1)
    low_half = lane < 64
    component = lax.rem(lane, 64)
    turn = jnp.where(low_half, 1.0, -1.0).astype(jnp.float32)

    def spread(to, value):
        for pair in range(LY // 2):
            same = value[:, :, 128 * pair : 128 * (pair + 1)]
            other = pltpu.roll(same, 64, 2)
            for t in range(LX // 2):
                for y in range(2):
                    a, b = (same, other) if y == 0 else (other, same)
                    fields[to, :, t, pl.ds(2 * pair + y, 1)] = jnp.where(
                        low_half[None], a[:, 2 * t : 2 * t + 1], b[:, 2 * t + 1 : 2 * t + 2])

    def collapse(ref, c, same):
        other = pltpu.roll(same, 64, 2)
        for t in range(LX // 2):
            for x in range(2):
                a, b = (same, other) if x == 0 else (other, same)
                for pair in range(LY // 2):
                    ref[c, pl.ds(2 * t + x, 1), 128 * pair : 128 * (pair + 1)] = jnp.where(
                        low_half, a[t, 2 * pair : 2 * pair + 1], b[t, 2 * pair + 1 : 2 * pair + 2])

    spread(0, magnet[...])
    wide[:, :, 0:3, 1] = jnp.zeros((1 + STEPS, 3, 3, LY, 128), jnp.float32)
    wide[:, :, 5:8, 1] = jnp.zeros((1 + STEPS, 3, 3, LY, 128), jnp.float32)

    barrier = pltpu.get_barrier_semaphore()
    diagonal = [(dx, dy) for dx, dy in OFFSETS if dx and dy]
    for i in range(1, nx):
        pl.semaphore_signal(barrier, 1, device_id=(lax.rem(me_x + i, nx), me_y), device_id_type=MESH)
    for i in range(1, ny):
        pl.semaphore_signal(barrier, 1, device_id=(me_x, lax.rem(me_y + i, ny)), device_id_type=MESH)
    for dx, dy in diagonal:
        @pl.when(present(dx, dy))
        def _():
            pl.semaphore_signal(barrier, 1, device_id=(me_x + dx, me_y + dy), device_id_type=MESH)
    beside_x = jnp.minimum(me_x, 2) + jnp.minimum(nx - 1 - me_x, 2)
    beside_y = jnp.minimum(me_y, 1) + jnp.minimum(ny - 1 - me_y, 1)
    pl.semaphore_wait(barrier, nx + ny - 2 + beside_x * beside_y)

    def along_y(i, src, dst, send, recv):
        return pltpu.make_async_remote_copy(
            src, dst, send.at[i], recv.at[i],
            device_id=(me_x, lax.rem(me_y + i, ny)), device_id_type=MESH)

    def along_x(i, src, dst, send, recv):
        return pltpu.make_async_remote_copy(
            src, dst, send.at[i], recv.at[i],
            device_id=(lax.rem(me_x + i, nx), me_y), device_id_type=MESH)

    gather = [along_y(i, fields.at[0], rows_in.at[me_y], ag_send, ag_recv) for i in range(1, ny)]
    for copy in gather:
        copy.start()

    def side(i):
        if i < 4:
            d = (-2, -1, 1, 2)[i]
            at, first, count = PLACE[-d]
            many = 2 if abs(d) == 2 else 1 + STEPS
            src = fields.at[pl.ds(0, many), :, pl.ds(first, count)]
            dst = wide.at[pl.ds(0, many), :, pl.ds(at, count), 1]
            return d, 0, src, dst
        d = (-1, 1)[i - 4]
        return 0, d, wide.at[:, :, :, 1], wide.at[:, :, :, 1 - d]

    def side_copy(i):
        dx, dy, src, dst = side(i)
        return pltpu.make_async_remote_copy(
            src, dst, side_send.at[i], side_recv.at[i],
            device_id=(me_x + dx, me_y + dy), device_id_type=MESH)

    def side_start(which):
        for i in which:
            @pl.when(present(*side(i)[:2]))
            def _():
                side_copy(i).start()

    def side_wait(which):
        for i in which:
            dx, dy = side(i)[:2]

            @pl.when(present(dx, dy))
            def _():
                side_copy(i).wait_send()

            @pl.when(present(-dx, -dy))
            def _():
                side_copy(i).wait_recv()

    def halo(i):
        dx, dy = OFFSETS[i]
        at, first, count = PLACE[-dx]
        return pltpu.make_async_remote_copy(
            demag.at[:, pl.ds(first, count)], wide_demag.at[:, pl.ds(at, count), 1 - dy],
            dem_send.at[i], dem_recv.at[i],
            device_id=(me_x + dx, me_y + dy), device_id_type=MESH)

    for s in range(STEPS):
        spread(1 + s, thermal[s])
    side_start(range(4))
    wide[0:4, :, 3:5, 1] = fields[...]
    rows_in[me_y] = fields[0]

    for i in (2, 3, 4):
        loads[i].wait()
    for y in range(8):
        for source, first, last in ((diag, 0, 128), (off, 128, 384)):
            piece = source[:, :, y, :].reshape(3 * block, 2 * x_all)
            high, low = split(piece)
            both = jnp.concatenate([high, low], axis=0)
            tensor[pl.ds(y * 2 * x_all, 2 * x_all), first:last] = lax.dot_general(
                both, place[:, first:last], (((0,), (0,)), ((), ())), preferred_element_type=jnp.float32)

    loads[1].wait()
    z_fwd[...] = jnp.zeros_like(z_fwd)
    for x in range(2):
        for part in range(6):
            z_fwd[:, pl.ds(128 * part + NZ * x, NZ), 128 * x : 128 * (x + 1)] = z_small[:, pl.ds(NZ * part, NZ)]
    loads[5].wait()
    for a in range(8):
        own = lax.rem(lax.broadcasted_iota(jnp.int32, (1, 1, 8 * x_all), 2), 8) == a
        own = jnp.where(own, 1.0, 0.0).astype(jnp.bfloat16)
        for part in range(2):
            x_fwd[:, pl.ds((part * 8 + a) * 2 * x_all, 2 * x_all)] = (
                x_small[:, pl.ds(part * 2 * x_all, 2 * x_all)] * own)
    loads[0].wait()
    for copy in gather:
        copy.wait()
    data = jnp.concatenate(
        [rows_in[:, c, t].reshape(y_all, 128) for c in range(3) for t in range(2)], axis=1)
    spectrum = dot_left(y_fwd, data)
    for t in range(2):
        parts = []
        for c in range(3):
            lanes = slice((2 * c + t) * 128, (2 * c + t + 1) * 128)
            parts += [spectrum[: 2 * y_all, lanes], spectrum[2 * y_all :, lanes]]
        planes = dot_right(jnp.concatenate(parts, axis=1), z_fwd)
        for x in range(2):
            spec_out[:, 2 * t + x] = planes[:, x * 128 : (x + 1) * 128].reshape(nx, 8, 128)
    forward = [
        along_x(i, spec_out.at[lax.rem(me_x + i, nx)], spec_in.at[me_x], fwd_send, fwd_recv)
        for i in range(1, nx)
    ]
    for copy in forward:
        copy.start()
    spec_in[me_x] = spec_out[me_x]
    loads[6].wait()
    for copy in forward:
        copy.wait()
    side_wait(range(4))
    side_start((4, 5))

    size = 8 * 2 * x_all
    both = dot_left(x_fwd, spec_in[...].reshape(x_all * 8, 128))
    spectra = both[:size] + turn * pltpu.roll(both[size:], 64, 1)
    second = jnp.where(component < 2 * kept, pltpu.roll(spectra, 128 - kept, 1), pltpu.roll(spectra, 2 * kept, 1))
    third = jnp.where(component < kept, pltpu.roll(spectra, 128 - 2 * kept, 1), pltpu.roll(spectra, kept, 1))
    response = tensor[:, :128] * spectra + tensor[:, 128:256] * second + tensor[:, 256:] * third
    both = dot_left(x_inv, response)
    back = both[: x_all * 8] - turn * pltpu.roll(both[x_all * 8 :], 64, 1)
    back_out[...] = back.reshape(nx, LX, 8, 128)
    inverse = [
        along_x(i, back_out.at[lax.rem(me_x + i, nx)], back_in.at[me_x], inv_send, inv_recv)
        for i in range(1, nx)
    ]
    for copy in inverse:
        copy.start()
    back_in[me_x] = back_out[me_x]
    loads[7].wait()
    loads[8].wait()
    for copy in inverse:
        copy.wait()
    data = jnp.concatenate([back_in[:, x].reshape(nx * 8, 128) for x in range(LX)], axis=1)
    both = dot_left(y_inv, data)
    for x in range(LX):
        lanes = slice(x * 128, (x + 1) * 128)
        rows = both[:y_all, lanes] - turn * pltpu.roll(both[y_all:, lanes], 64, 1)
        row_out[:, x] = rows.reshape(ny, LY, 128)
    final = [
        along_y(i, row_out.at[lax.rem(me_y + i, ny)], row_in.at[me_y], last_send, last_recv)
        for i in range(1, ny)
    ]
    for copy in final:
        copy.start()
    row_in[me_y] = row_out[me_y]
    for copy in final:
        copy.wait()
    data = jnp.concatenate([row_in[g].reshape(LX * LY, 128) for g in range(ny)], axis=1)
    rows = dot_right(data, z_inv)
    turned = jnp.concatenate(
        [pltpu.roll(rows[:, :128], 64, 1), pltpu.roll(rows[:, 128:], 64, 1)], axis=1)
    for c, (a, b, first) in enumerate(((rows, turned, 0), (turned, rows, 0), (rows, turned, 128))):
        a, b = a[:, first : first + 128], b[:, first : first + 128]
        for t in range(2):
            demag[c, t] = jnp.where(low_half, a[16 * t : 16 * t + 8], b[16 * t + 8 : 16 * t + 16])
    for i, (dx, dy) in enumerate(OFFSETS):
        @pl.when(present(dx, dy))
        def _():
            halo(i).start()
    wide_demag[:, 3:5, 1] = demag[...]
    for c in range(3):
        collapse(demag_ref, c, demag[c])
    side_wait((4, 5))
    for i, (dx, dy) in enumerate(OFFSETS):
        @pl.when(present(dx, dy))
        def _():
            halo(i).wait_send()

        @pl.when(present(-dx, -dy))
        def _():
            halo(i).wait_recv()

    shape = (8, 3 * LY, 128)
    lanes = lax.broadcasted_iota(jnp.int32, shape, 2)
    x_at = LX * me_x - 6 + 2 * lax.broadcasted_iota(jnp.int32, shape, 0) + lanes // 64
    y_at = LY * me_y - LY + lax.broadcasted_iota(jnp.int32, shape, 1)
    z_at = lax.rem(lanes, 64)
    left_half = lanes < 64
    at_x0, at_x1 = x_at == 0, x_at == x_all - 1
    at_y0, at_y1 = y_at == 0, y_at == y_all - 1
    at_z0, at_z1 = z_at == 0, z_at == NZ - 1

    def laplace(v):
        turned = pltpu.roll(v, 64, 2)
        up = jnp.where(left_half, turned, jnp.concatenate([turned[1:], turned[-1:]], axis=0))
        down = jnp.where(left_half, jnp.concatenate([turned[:1], turned[:-1]], axis=0), turned)
        total = jnp.where(at_x1, v, up) + jnp.where(at_x0, v, down)
        total = total + jnp.where(at_y1, v, pltpu.roll(v, 3 * LY - 1, 1))
        total = total + jnp.where(at_y0, v, pltpu.roll(v, 1, 1))
        total = total + jnp.where(at_z1, v, pltpu.roll(v, 127, 2))
        total = total + jnp.where(at_z0, v, pltpu.roll(v, 1, 2))
        return total - 6.0 * v

    def torque(v, noise):
        h = [laplace(v[c]) + noise[c] for c in range(3)]
        h[2] = h[2] + ANISOTROPY * v[2]
        first = cross(v, h)
        second = cross(v, first)
        return [(first[c] + DAMPING * second[c]) * (-1.0 / (1.0 + DAMPING * DAMPING)) for c in range(3)]

    m = [wide[0, c].reshape(shape) for c in range(3)]
    for s in range(STEPS):
        noise = [wide_demag[c].reshape(shape) + wide[1 + s, c].reshape(shape) for c in range(3)]
        f0 = torque(m, noise)
        f1 = torque([m[c] + TIME_STEP * f0[c] for c in range(3)], noise)
        u = [m[c] + 0.5 * TIME_STEP * (f0[c] + f1[c]) for c in range(3)]
        norm = jnp.sqrt(u[0] * u[0] + u[1] * u[1] + u[2] * u[2])
        m = [u[c] / norm for c in range(3)]
    for c in range(3):
        collapse(final_ref, c, m[c][3:5, LY : 2 * LY])


def body(nx, ny, magnet, thermal, kernel_diag, kernel_off):
    block = 2 * NZ // ny
    x_all, y_all = nx * LX, ny * LY
    consts = tables(nx, ny)
    vmem = pl.BlockSpec(memory_space=pltpu.VMEM)
    anyspace = pl.BlockSpec(memory_space=pl.ANY)
    out = jax.ShapeDtypeStruct(magnet.shape, jnp.float32)
    f32, bf16 = jnp.float32, jnp.bfloat16
    scratch = [
        pltpu.VMEM((1 + STEPS, 3, LX // 2, LY, 128), f32),
        pltpu.VMEM((3, LX // 2, LY, 128), f32),
        pltpu.VMEM(kernel_diag.shape, f32),
        pltpu.VMEM(kernel_off.shape, f32),
        pltpu.VMEM(consts[0].shape, bf16),
        pltpu.VMEM(consts[1].shape[1:], bf16),
        pltpu.VMEM((2, 3 * 2 * 2 * NZ, 256), bf16),
        pltpu.VMEM(consts[2].shape, bf16),
        pltpu.VMEM((2, 2 * 8 * 2 * x_all, 8 * x_all), bf16),
        *[pltpu.VMEM(c.shape, bf16) for c in consts[3:]],
        pltpu.VMEM((1 + STEPS, 3, 8, 3, LY, 128), f32),
        pltpu.VMEM((3, 8, 3, LY, 128), f32),
        pltpu.VMEM((ny, 3, 2, LY, 128), f32),
        *[pltpu.VMEM((nx, LX, 8, 128), f32)] * 4,
        *[pltpu.VMEM((ny, LX, LY, 128), f32)] * 2,
        pltpu.VMEM((8 * 2 * x_all, 384), f32),
        pltpu.SemaphoreType.DMA((9,)),
        *[pltpu.SemaphoreType.DMA((6,))] * 2,
        *[pltpu.SemaphoreType.DMA((len(OFFSETS),))] * 2,
        *[pltpu.SemaphoreType.DMA((ny,))] * 2,
        *[pltpu.SemaphoreType.DMA((nx,))] * 4,
        *[pltpu.SemaphoreType.DMA((ny,))] * 2,
    ]
    return pl.pallas_call(
        functools.partial(kernel, nx, ny),
        out_shape=(out, out),
        in_specs=[vmem, vmem] + [anyspace] * 9,
        out_specs=(vmem, vmem),
        scratch_shapes=scratch,
        compiler_params=pltpu.CompilerParams(
            collective_id=0, has_side_effects=True, vmem_limit_bytes=56 * 1024 * 1024),
    )(magnet, thermal, kernel_diag, kernel_off, *[jnp.asarray(c) for c in consts])


def solution(mesh):
    in_specs = (
        P(None, "gx", "gy"),
        P(None, None, "gx", "gy"),
        P(None, "gy", "gx", None),
        P(None, "gy", "gx", None),
    )
    out_specs = (P(None, "gx", "gy"), P(None, "gx", "gy"))
    run = functools.partial(body, mesh.shape["gx"], mesh.shape["gy"])
    return jax.shard_map(run, mesh=mesh, in_specs=in_specs, out_specs=out_specs, check_vma=False)
```

```python
import functools

import jax
import jax.numpy as jnp
import ml_dtypes
import numpy as np
from jax import lax
from jax.experimental import pallas as pl
from jax.experimental.pallas import tpu as pltpu
from jax.sharding import PartitionSpec as P

NZ = 64
STEPS = 3
DAMPING = 0.1
TIME_STEP = 0.05
ANISOTROPY = 0.5
LX = 4
LY = 8
MESH = pl.DeviceIdType.MESH
OFFSETS = [(dx, dy) for dx in (-2, -1, 0, 1, 2) for dy in (-1, 0, 1) if (dx, dy) != (0, 0)]
PLACE = {-2: (0, 1, 1), -1: (1, 0, 2), 0: (3, 0, 2), 1: (5, 0, 2), 2: (7, 0, 1)}


def halves(table):
    table = np.asarray(table, np.float32)
    high = table.astype(ml_dtypes.bfloat16)
    low = (table - high.astype(np.float32)).astype(ml_dtypes.bfloat16)
    return np.stack([high, low])


def beside(table):
    high, low = halves(table)
    return np.concatenate([high, low, high], axis=1)


def angles(first, second, period):
    return 2.0 * np.pi * ((np.asarray(first)[:, None] * np.asarray(second)[None, :]) % period) / period


def tables(nx, ny):
    x_all, y_all = nx * LX, ny * LY
    block = 2 * NZ // ny
    kept = block // 2 + 1
    ang = angles(np.arange(2 * y_all), np.arange(y_all), 2 * y_all)
    y_fwd = np.concatenate([np.cos(ang), -np.sin(ang)])
    z_fwd = np.zeros((ny, 3, 2, NZ, 128))
    z_inv = np.zeros((ny, 128, 4, NZ))
    for g in range(ny):
        kz = g * block + np.arange(kept)
        ang = angles(np.arange(NZ), kz, 2 * NZ)
        weight = np.full((kept,), 2.0)
        if g in (0, ny // 2):
            weight[0] = 1.0
        if g > ny // 2:
            weight[0] = 0.0
        if g < ny // 2:
            weight[kept - 1] = 0.0
        weight = -weight / (8.0 * x_all * y_all * NZ)
        for c in range(3):
            re = slice(c * kept, (c + 1) * kept)
            im = slice(64 + c * kept, 64 + (c + 1) * kept)
            z_fwd[g, c, 0, :, re] = np.cos(ang)
            z_fwd[g, c, 1, :, re] = np.sin(ang)
            z_fwd[g, c, 1, :, im] = np.cos(ang)
            z_fwd[g, c, 0, :, im] = -np.sin(ang)
            z_inv[g, re, c] = (np.cos(ang) * weight).T
            z_inv[g, im, c] = (-np.sin(ang) * weight).T
    z_fwd = z_fwd.reshape(ny, 3 * 2 * NZ, 128)
    z_inv = z_inv.reshape(ny * 128, 4 * NZ)
    ang = angles(np.arange(2 * x_all), np.arange(x_all), 2 * x_all)
    eye = np.eye(8)
    x_fwd = np.stack([np.cos(ang), np.sin(ang)])
    x_inv = np.einsum("skx,ab->sxabk", x_fwd, eye).reshape(2 * x_all * 8, 8 * 2 * x_all)
    x_fwd = np.repeat(x_fwd.reshape(2 * 2 * x_all, x_all), 8, axis=1)
    ang = angles(np.arange(y_all), np.arange(2 * y_all), 2 * y_all)
    y_inv = np.concatenate([np.cos(ang), np.sin(ang)])
    place = np.zeros((3, 2, 3, block, 128))
    pairs = {(0, 1): 0, (0, 2): 1, (1, 2): 2}
    for c in range(3):
        for d in range(3):
            other = (c + d) % 3
            entry = c if d == 0 else pairs[(min(c, other), max(c, other))]
            for half in range(2):
                for j in range(kept):
                    place[d, :, entry, j, half * 64 + c * kept + j] = 1.0
    place = place.reshape(3, 6 * block, 128)
    place = np.concatenate([place[0], place[1], place[2]], axis=1).astype(ml_dtypes.bfloat16)
    return (
        beside(y_fwd),
        np.moveaxis(halves(z_fwd), 0, 1),
        halves(x_fwd),
        halves(x_inv),
        beside(y_inv),
        halves(z_inv),
        place,
    )


def split(value):
    high = value.astype(jnp.bfloat16)
    low = (value - high.astype(jnp.float32)).astype(jnp.bfloat16)
    return high, low


def dot(left, right):
    return jnp.dot(left, right, preferred_element_type=jnp.float32)


def dot_left(table, data):
    high, low = split(data)
    both = dot(table[0], jnp.concatenate([high, low], axis=1))
    lanes = data.shape[1]
    return both[:, :lanes] + (both[:, lanes:] + dot(table[1], high))


def dot_thin(table, data):
    high, low = split(data)
    return dot(table[...], jnp.concatenate([high, high, low], axis=0))


def dot_right(data, table):
    high, low = split(data)
    both = dot(jnp.concatenate([high, low], axis=0), table[0])
    rows = data.shape[0]
    return both[:rows] + (both[rows:] + dot(high, table[1]))


def cross(a, b):
    return [a[1] * b[2] - a[2] * b[1], a[2] * b[0] - a[0] * b[2], a[0] * b[1] - a[1] * b[0]]


def kernel(
    nx, ny,
    magnet, thermal, diag_h, off_h, y_fwd_h, z_fwd_h, x_fwd_h, x_inv_h, y_inv_h, z_inv_h, place_h,
    final_ref, demag_ref,
    fields, demag, diag, off, y_fwd, z_small, z_fwd, x_small, x_fwd, x_inv, y_inv, z_inv, place,
    wide, wide_demag, rows_in, spec_out, spec_in, back_out, back_in, row_out, row_in, tensor,
    local_sem, side_send, side_recv, dem_send, dem_recv, ag_send, ag_recv,
    fwd_send, fwd_recv, inv_send, inv_recv, last_send, last_recv,
):
    x_all, y_all = nx * LX, ny * LY
    block = 2 * NZ // ny
    kept = block // 2 + 1
    me_x, me_y = lax.axis_index("gx"), lax.axis_index("gy")

    loads = [
        pltpu.make_async_copy(src, dst, local_sem.at[i])
        for i, (src, dst) in enumerate([
            (y_fwd_h, y_fwd), (z_fwd_h.at[me_y], z_small), (diag_h, diag), (off_h, off),
            (place_h, place), (x_fwd_h, x_small), (x_inv_h, x_inv), (y_inv_h, y_inv), (z_inv_h, z_inv),
        ])
    ]
    for load in loads:
        load.start()

    def present(dx, dy):
        x, y = me_x + dx, me_y + dy
        return (x >= 0) & (x < nx) & (y >= 0) & (y < ny)

    lane = lax.broadcasted_iota(jnp.int32, (1, 128), 1)
    low_half = lane < 64
    component = lax.rem(lane, 64)
    turn = jnp.where(low_half, 1.0, -1.0).astype(jnp.float32)

    def spread(to, value):
        for pair in range(LY // 2):
            same = value[:, :, 128 * pair : 128 * (pair + 1)]
            other = pltpu.roll(same, 64, 2)
            for t in range(LX // 2):
                for y in range(2):
                    a, b = (same, other) if y == 0 else (other, same)
                    fields[to, :, t, pl.ds(2 * pair + y, 1)] = jnp.where(
                        low_half[None], a[:, 2 * t : 2 * t + 1], b[:, 2 * t + 1 : 2 * t + 2])

    def collapse(ref, c, same):
        other = pltpu.roll(same, 64, 2)
        for t in range(LX // 2):
            for x in range(2):
                a, b = (same, other) if x == 0 else (other, same)
                for pair in range(LY // 2):
                    ref[c, pl.ds(2 * t + x, 1), 128 * pair : 128 * (pair + 1)] = jnp.where(
                        low_half, a[t, 2 * pair : 2 * pair + 1], b[t, 2 * pair + 1 : 2 * pair + 2])

    spread(0, magnet[...])
    wide[:, :, 0:3, 1] = jnp.zeros((1 + STEPS, 3, 3, LY, 128), jnp.float32)
    wide[:, :, 5:8, 1] = jnp.zeros((1 + STEPS, 3, 3, LY, 128), jnp.float32)

    barrier = pltpu.get_barrier_semaphore()
    diagonal = [(dx, dy) for dx, dy in OFFSETS if dx and dy]
    for i in range(1, nx):
        pl.semaphore_signal(barrier, 1, device_id=(lax.rem(me_x + i, nx), me_y), device_id_type=MESH)
    for i in range(1, ny):
        pl.semaphore_signal(barrier, 1, device_id=(me_x, lax.rem(me_y + i, ny)), device_id_type=MESH)
    for dx, dy in diagonal:
        @pl.when(present(dx, dy))
        def _():
            pl.semaphore_signal(barrier, 1, device_id=(me_x + dx, me_y + dy), device_id_type=MESH)
    beside_x = jnp.minimum(me_x, 2) + jnp.minimum(nx - 1 - me_x, 2)
    beside_y = jnp.minimum(me_y, 1) + jnp.minimum(ny - 1 - me_y, 1)
    pl.semaphore_wait(barrier, nx + ny - 2 + beside_x * beside_y)

    def along_y(i, src, dst, send, recv):
        return pltpu.make_async_remote_copy(
            src, dst, send.at[i], recv.at[i],
            device_id=(me_x, lax.rem(me_y + i, ny)), device_id_type=MESH)

    def along_x(i, src, dst, send, recv):
        return pltpu.make_async_remote_copy(
            src, dst, send.at[i], recv.at[i],
            device_id=(lax.rem(me_x + i, nx), me_y), device_id_type=MESH)

    far_first = sorted(range(1, nx), key=lambda i: abs(2 * i - nx))

    gather = [along_y(i, fields.at[0], rows_in.at[me_y], ag_send, ag_recv) for i in range(1, ny)]
    for copy in gather:
        copy.start()

    def side(i):
        if i < 4:
            d = (-2, -1, 1, 2)[i]
            at, first, count = PLACE[-d]
            many = 2 if abs(d) == 2 else 1 + STEPS
            src = fields.at[pl.ds(0, many), :, pl.ds(first, count)]
            dst = wide.at[pl.ds(0, many), :, pl.ds(at, count), 1]
            return d, 0, src, dst
        d = (-1, 1)[i - 4]
        return 0, d, wide.at[:, :, :, 1], wide.at[:, :, :, 1 - d]

    def side_copy(i):
        dx, dy, src, dst = side(i)
        return pltpu.make_async_remote_copy(
            src, dst, side_send.at[i], side_recv.at[i],
            device_id=(me_x + dx, me_y + dy), device_id_type=MESH)

    def side_start(which):
        for i in which:
            @pl.when(present(*side(i)[:2]))
            def _():
                side_copy(i).start()

    def side_wait(which):
        for i in which:
            dx, dy = side(i)[:2]

            @pl.when(present(dx, dy))
            def _():
                side_copy(i).wait_send()

            @pl.when(present(-dx, -dy))
            def _():
                side_copy(i).wait_recv()

    def halo(i):
        dx, dy = OFFSETS[i]
        at, first, count = PLACE[-dx]
        return pltpu.make_async_remote_copy(
            demag.at[:, pl.ds(first, count)], wide_demag.at[:, pl.ds(at, count), 1 - dy],
            dem_send.at[i], dem_recv.at[i],
            device_id=(me_x + dx, me_y + dy), device_id_type=MESH)

    for s in range(STEPS):
        spread(1 + s, thermal[s])
    side_start(range(4))
    wide[0:4, :, 3:5, 1] = fields[...]
    rows_in[me_y] = fields[0]

    loads[1].wait()
    z_fwd[...] = jnp.zeros_like(z_fwd)
    for x in range(2):
        for part in range(6):
            z_fwd[:, pl.ds(128 * part + NZ * x, NZ), 128 * x : 128 * (x + 1)] = z_small[:, pl.ds(NZ * part, NZ)]
    loads[0].wait()
    for copy in gather:
        copy.wait()
    data = jnp.concatenate(
        [rows_in[:, c, t].reshape(y_all, 128) for c in range(3) for t in range(2)], axis=1)
    spectrum = dot_thin(y_fwd, data)
    joined = []
    for t in range(2):
        parts = []
        for c in range(3):
            lanes = slice((2 * c + t) * 128, (2 * c + t + 1) * 128)
            parts += [spectrum[: 2 * y_all, lanes], spectrum[2 * y_all :, lanes]]
        joined.append(jnp.concatenate(parts, axis=1))
    planes = dot_right(jnp.concatenate(joined, axis=0), z_fwd)
    for t in range(2):
        for x in range(2):
            piece = planes[t * 2 * y_all : (t + 1) * 2 * y_all, x * 128 : (x + 1) * 128]
            spec_out[:, 2 * t + x] = piece.reshape(nx, 8, 128)
    forward = [
        along_x(i, spec_out.at[lax.rem(me_x + i, nx)], spec_in.at[me_x], fwd_send, fwd_recv)
        for i in far_first
    ]
    for copy in forward:
        copy.start()
    spec_in[me_x] = spec_out[me_x]

    for i in (2, 3, 4):
        loads[i].wait()
    for y in range(8):
        for source, first, last in ((diag, 0, 128), (off, 128, 384)):
            piece = source[:, :, y, :].reshape(3 * block, 2 * x_all)
            high, low = split(piece)
            both = jnp.concatenate([high, low], axis=0)
            tensor[pl.ds(y * 2 * x_all, 2 * x_all), first:last] = lax.dot_general(
                both, place[:, first:last], (((0,), (0,)), ((), ())), preferred_element_type=jnp.float32)
    loads[5].wait()
    for a in range(8):
        own = lax.rem(lax.broadcasted_iota(jnp.int32, (1, 1, 8 * x_all), 2), 8) == a
        own = jnp.where(own, 1.0, 0.0).astype(jnp.bfloat16)
        for part in range(2):
            x_fwd[:, pl.ds((part * 8 + a) * 2 * x_all, 2 * x_all)] = (
                x_small[:, pl.ds(part * 2 * x_all, 2 * x_all)] * own)
    loads[6].wait()
    for copy in forward:
        copy.wait()
    side_wait(range(4))
    side_start((4, 5))

    size = 8 * 2 * x_all
    both = dot_left(x_fwd, spec_in[...].reshape(x_all * 8, 128))
    spectra = both[:size] + turn * pltpu.roll(both[size:], 64, 1)
    second = jnp.where(component < 2 * kept, pltpu.roll(spectra, 128 - kept, 1), pltpu.roll(spectra, 2 * kept, 1))
    third = jnp.where(component < kept, pltpu.roll(spectra, 128 - 2 * kept, 1), pltpu.roll(spectra, kept, 1))
    response = tensor[:, :128] * spectra + tensor[:, 128:256] * second + tensor[:, 256:] * third
    both = dot_left(x_inv, response)
    back = both[: x_all * 8] - turn * pltpu.roll(both[x_all * 8 :], 64, 1)
    back_out[...] = back.reshape(nx, LX, 8, 128)
    inverse = [
        along_x(i, back_out.at[lax.rem(me_x + i, nx)], back_in.at[me_x], inv_send, inv_recv)
        for i in far_first
    ]
    for copy in inverse:
        copy.start()
    back_in[me_x] = back_out[me_x]
    loads[7].wait()
    loads[8].wait()
    for copy in inverse:
        copy.wait()
    data = jnp.concatenate([back_in[:, x].reshape(nx * 8, 128) for x in range(LX)], axis=1)
    both = dot_thin(y_inv, data)
    for x in range(LX):
        lanes = slice(x * 128, (x + 1) * 128)
        rows = both[:y_all, lanes] - turn * pltpu.roll(both[y_all:, lanes], 64, 1)
        row_out[:, x] = rows.reshape(ny, LY, 128)
    final = [
        along_y(i, row_out.at[lax.rem(me_y + i, ny)], row_in.at[me_y], last_send, last_recv)
        for i in range(1, ny)
    ]
    for copy in final:
        copy.start()
    row_in[me_y] = row_out[me_y]
    for copy in final:
        copy.wait()
    data = jnp.concatenate([row_in[g].reshape(LX * LY, 128) for g in range(ny)], axis=1)
    rows = dot_right(data, z_inv)
    turned = jnp.concatenate(
        [pltpu.roll(rows[:, :128], 64, 1), pltpu.roll(rows[:, 128:], 64, 1)], axis=1)
    for c, (a, b, first) in enumerate(((rows, turned, 0), (turned, rows, 0), (rows, turned, 128))):
        a, b = a[:, first : first + 128], b[:, first : first + 128]
        for t in range(2):
            demag[c, t] = jnp.where(low_half, a[16 * t : 16 * t + 8], b[16 * t + 8 : 16 * t + 16])
    for i, (dx, dy) in enumerate(OFFSETS):
        @pl.when(present(dx, dy))
        def _():
            halo(i).start()
    wide_demag[:, 3:5, 1] = demag[...]
    for c in range(3):
        collapse(demag_ref, c, demag[c])
    side_wait((4, 5))
    for i, (dx, dy) in enumerate(OFFSETS):
        @pl.when(present(dx, dy))
        def _():
            halo(i).wait_send()

        @pl.when(present(-dx, -dy))
        def _():
            halo(i).wait_recv()

    shape = (8, 3 * LY, 128)
    lanes = lax.broadcasted_iota(jnp.int32, shape, 2)
    x_at = LX * me_x - 6 + 2 * lax.broadcasted_iota(jnp.int32, shape, 0) + lanes // 64
    y_at = LY * me_y - LY + lax.broadcasted_iota(jnp.int32, shape, 1)
    z_at = lax.rem(lanes, 64)
    left_half = lanes < 64
    at_x0, at_x1 = x_at == 0, x_at == x_all - 1
    at_y0, at_y1 = y_at == 0, y_at == y_all - 1
    at_z0, at_z1 = z_at == 0, z_at == NZ - 1

    def laplace(v):
        turned = pltpu.roll(v, 64, 2)
        up = jnp.where(left_half, turned, jnp.concatenate([turned[1:], turned[-1:]], axis=0))
        down = jnp.where(left_half, jnp.concatenate([turned[:1], turned[:-1]], axis=0), turned)
        total = jnp.where(at_x1, v, up) + jnp.where(at_x0, v, down)
        total = total + jnp.where(at_y1, v, pltpu.roll(v, 3 * LY - 1, 1))
        total = total + jnp.where(at_y0, v, pltpu.roll(v, 1, 1))
        total = total + jnp.where(at_z1, v, pltpu.roll(v, 127, 2))
        total = total + jnp.where(at_z0, v, pltpu.roll(v, 1, 2))
        return total - 6.0 * v

    def torque(v, noise):
        h = [laplace(v[c]) + noise[c] for c in range(3)]
        h[2] = h[2] + ANISOTROPY * v[2]
        first = cross(v, h)
        second = cross(v, first)
        return [(first[c] + DAMPING * second[c]) * (-1.0 / (1.0 + DAMPING * DAMPING)) for c in range(3)]

    m = [wide[0, c].reshape(shape) for c in range(3)]
    for s in range(STEPS):
        noise = [wide_demag[c].reshape(shape) + wide[1 + s, c].reshape(shape) for c in range(3)]
        f0 = torque(m, noise)
        f1 = torque([m[c] + TIME_STEP * f0[c] for c in range(3)], noise)
        u = [m[c] + 0.5 * TIME_STEP * (f0[c] + f1[c]) for c in range(3)]
        norm = jnp.sqrt(u[0] * u[0] + u[1] * u[1] + u[2] * u[2])
        m = [u[c] / norm for c in range(3)]
    for c in range(3):
        collapse(final_ref, c, m[c][3:5, LY : 2 * LY])


def body(nx, ny, magnet, thermal, kernel_diag, kernel_off):
    block = 2 * NZ // ny
    x_all, y_all = nx * LX, ny * LY
    consts = tables(nx, ny)
    vmem = pl.BlockSpec(memory_space=pltpu.VMEM)
    anyspace = pl.BlockSpec(memory_space=pl.ANY)
    out = jax.ShapeDtypeStruct(magnet.shape, jnp.float32)
    f32, bf16 = jnp.float32, jnp.bfloat16
    scratch = [
        pltpu.VMEM((1 + STEPS, 3, LX // 2, LY, 128), f32),
        pltpu.VMEM((3, LX // 2, LY, 128), f32),
        pltpu.VMEM(kernel_diag.shape, f32),
        pltpu.VMEM(kernel_off.shape, f32),
        pltpu.VMEM(consts[0].shape, bf16),
        pltpu.VMEM(consts[1].shape[1:], bf16),
        pltpu.VMEM((2, 3 * 2 * 2 * NZ, 256), bf16),
        pltpu.VMEM(consts[2].shape, bf16),
        pltpu.VMEM((2, 2 * 8 * 2 * x_all, 8 * x_all), bf16),
        *[pltpu.VMEM(c.shape, bf16) for c in consts[3:]],
        pltpu.VMEM((1 + STEPS, 3, 8, 3, LY, 128), f32),
        pltpu.VMEM((3, 8, 3, LY, 128), f32),
        pltpu.VMEM((ny, 3, 2, LY, 128), f32),
        *[pltpu.VMEM((nx, LX, 8, 128), f32)] * 4,
        *[pltpu.VMEM((ny, LX, LY, 128), f32)] * 2,
        pltpu.VMEM((8 * 2 * x_all, 384), f32),
        pltpu.SemaphoreType.DMA((9,)),
        *[pltpu.SemaphoreType.DMA((6,))] * 2,
        *[pltpu.SemaphoreType.DMA((len(OFFSETS),))] * 2,
        *[pltpu.SemaphoreType.DMA((ny,))] * 2,
        *[pltpu.SemaphoreType.DMA((nx,))] * 4,
        *[pltpu.SemaphoreType.DMA((ny,))] * 2,
    ]
    return pl.pallas_call(
        functools.partial(kernel, nx, ny),
        out_shape=(out, out),
        in_specs=[vmem, vmem] + [anyspace] * 9,
        out_specs=(vmem, vmem),
        scratch_shapes=scratch,
        compiler_params=pltpu.CompilerParams(
            collective_id=0, has_side_effects=True, vmem_limit_bytes=56 * 1024 * 1024),
    )(magnet, thermal, kernel_diag, kernel_off, *[jnp.asarray(c) for c in consts])


def solution(mesh):
    in_specs = (
        P(None, "gx", "gy"),
        P(None, None, "gx", "gy"),
        P(None, "gy", "gx", None),
        P(None, "gy", "gx", None),
    )
    out_specs = (P(None, "gx", "gy"), P(None, "gx", "gy"))
    run = functools.partial(body, mesh.shape["gx"], mesh.shape["gy"])
    return jax.shard_map(run, mesh=mesh, in_specs=in_specs, out_specs=out_specs, check_vma=False)
```

```python
import functools

import jax
import jax.numpy as jnp
import ml_dtypes
import numpy as np
from jax import lax
from jax.experimental import pallas as pl
from jax.experimental.pallas import tpu as pltpu
from jax.sharding import PartitionSpec as P

NZ = 64
STEPS = 3
DAMPING = 0.1
TIME_STEP = 0.05
ANISOTROPY = 0.5
LX = 4
LY = 8
MESH = pl.DeviceIdType.MESH
OFFSETS = [(dx, dy) for dx in (-2, -1, 0, 1, 2) for dy in (-1, 0, 1) if (dx, dy) != (0, 0)]
PLACE = {-2: (0, 1, 1), -1: (1, 0, 2), 0: (3, 0, 2), 1: (5, 0, 2), 2: (7, 0, 1)}


def halves(table):
    table = np.asarray(table, np.float32)
    high = table.astype(ml_dtypes.bfloat16)
    low = (table - high.astype(np.float32)).astype(ml_dtypes.bfloat16)
    return np.stack([high, low])


def beside(table):
    high, low = halves(table)
    return np.concatenate([high, low, high], axis=1)


def angles(first, second, period):
    return 2.0 * np.pi * ((np.asarray(first)[:, None] * np.asarray(second)[None, :]) % period) / period


def tables(nx, ny):
    x_all, y_all = nx * LX, ny * LY
    block = 2 * NZ // ny
    kept = block // 2 + 1
    ang = angles(np.arange(2 * y_all), np.arange(y_all), 2 * y_all)
    y_fwd = np.concatenate([np.cos(ang), -np.sin(ang)])
    z_fwd = np.zeros((ny, 3, 2, NZ, 128))
    z_inv = np.zeros((ny, 128, 4, NZ))
    for g in range(ny):
        kz = g * block + np.arange(kept)
        ang = angles(np.arange(NZ), kz, 2 * NZ)
        weight = np.full((kept,), 2.0)
        if g in (0, ny // 2):
            weight[0] = 1.0
        if g > ny // 2:
            weight[0] = 0.0
        if g < ny // 2:
            weight[kept - 1] = 0.0
        weight = -weight / (8.0 * x_all * y_all * NZ)
        for c in range(3):
            re = slice(c * kept, (c + 1) * kept)
            im = slice(64 + c * kept, 64 + (c + 1) * kept)
            z_fwd[g, c, 0, :, re] = np.cos(ang)
            z_fwd[g, c, 1, :, re] = np.sin(ang)
            z_fwd[g, c, 1, :, im] = np.cos(ang)
            z_fwd[g, c, 0, :, im] = -np.sin(ang)
            z_inv[g, re, c] = (np.cos(ang) * weight).T
            z_inv[g, im, c] = (-np.sin(ang) * weight).T
    z_fwd = z_fwd.reshape(ny, 3 * 2 * NZ, 128)
    z_inv = z_inv.reshape(ny * 128, 4 * NZ)
    ang = angles(np.arange(2 * x_all), np.arange(x_all), 2 * x_all)
    eye = np.eye(8)
    x_fwd = np.stack([np.cos(ang), np.sin(ang)])
    x_inv = np.einsum("skx,ab->sxabk", x_fwd, eye).reshape(2 * x_all * 8, 8 * 2 * x_all)
    x_fwd = np.repeat(x_fwd.reshape(2 * 2 * x_all, x_all), 8, axis=1)
    ang = angles(np.arange(y_all), np.arange(2 * y_all), 2 * y_all)
    y_inv = np.concatenate([np.cos(ang), np.sin(ang)])
    place = np.zeros((3, 2, 3, block, 128))
    pairs = {(0, 1): 0, (0, 2): 1, (1, 2): 2}
    for c in range(3):
        for d in range(3):
            other = (c + d) % 3
            entry = c if d == 0 else pairs[(min(c, other), max(c, other))]
            for half in range(2):
                for j in range(kept):
                    place[d, :, entry, j, half * 64 + c * kept + j] = 1.0
    place = place.reshape(3, 6 * block, 128)
    place = np.concatenate([place[0], place[1], place[2]], axis=1).astype(ml_dtypes.bfloat16)
    return (
        beside(y_fwd),
        np.moveaxis(halves(z_fwd), 0, 1),
        halves(x_fwd),
        halves(x_inv),
        beside(y_inv),
        halves(z_inv),
        place,
    )


def split(value):
    high = value.astype(jnp.bfloat16)
    low = (value - high.astype(jnp.float32)).astype(jnp.bfloat16)
    return high, low


def dot(left, right):
    return jnp.dot(left, right, preferred_element_type=jnp.float32)


def dot_left(table, data):
    high, low = split(data)
    both = dot(table[0], jnp.concatenate([high, low], axis=1))
    lanes = data.shape[1]
    return both[:, :lanes] + (both[:, lanes:] + dot(table[1], high))


def dot_thin(table, data):
    high, low = split(data)
    return dot(table[...], jnp.concatenate([high, high, low], axis=0))


def dot_right(data, table):
    high, low = split(data)
    both = dot(jnp.concatenate([high, low], axis=0), table[0])
    rows = data.shape[0]
    return both[:rows] + (both[rows:] + dot(high, table[1]))


def cross(a, b):
    return [a[1] * b[2] - a[2] * b[1], a[2] * b[0] - a[0] * b[2], a[0] * b[1] - a[1] * b[0]]


def kernel(
    nx, ny,
    magnet, thermal, diag_h, off_h, y_fwd_h, z_fwd_h, x_fwd_h, x_inv_h, y_inv_h, z_inv_h, place_h,
    final_ref, demag_ref,
    fields, demag, diag, off, y_fwd, z_small, z_fwd, x_small, x_fwd, x_inv, y_inv, z_inv, place,
    wide, wide_demag, rows_in, spec_out, spec_in, back_out, back_in, row_out, row_in, tensor,
    local_sem, side_send, side_recv, dem_send, dem_recv, ag_send, ag_recv,
    fwd_send, fwd_recv, inv_send, inv_recv, last_send, last_recv,
):
    x_all, y_all = nx * LX, ny * LY
    block = 2 * NZ // ny
    kept = block // 2 + 1
    me_x, me_y = lax.axis_index("gx"), lax.axis_index("gy")

    loads = [
        pltpu.make_async_copy(src, dst, local_sem.at[i])
        for i, (src, dst) in enumerate([
            (y_fwd_h, y_fwd), (z_fwd_h.at[me_y], z_small), (diag_h, diag), (off_h, off),
            (place_h, place), (x_fwd_h, x_small), (x_inv_h, x_inv), (y_inv_h, y_inv), (z_inv_h, z_inv),
        ])
    ]
    for i in (1, 0):
        loads[i].start()

    def present(dx, dy):
        x, y = me_x + dx, me_y + dy
        return (x >= 0) & (x < nx) & (y >= 0) & (y < ny)

    lane = lax.broadcasted_iota(jnp.int32, (1, 128), 1)
    low_half = lane < 64
    component = lax.rem(lane, 64)
    turn = jnp.where(low_half, 1.0, -1.0).astype(jnp.float32)

    def spread(to, value):
        for pair in range(LY // 2):
            same = value[:, :, 128 * pair : 128 * (pair + 1)]
            other = pltpu.roll(same, 64, 2)
            for t in range(LX // 2):
                for y in range(2):
                    a, b = (same, other) if y == 0 else (other, same)
                    fields[to, :, t, pl.ds(2 * pair + y, 1)] = jnp.where(
                        low_half[None], a[:, 2 * t : 2 * t + 1], b[:, 2 * t + 1 : 2 * t + 2])

    def collapse(ref, c, same):
        other = pltpu.roll(same, 64, 2)
        for t in range(LX // 2):
            for x in range(2):
                a, b = (same, other) if x == 0 else (other, same)
                for pair in range(LY // 2):
                    ref[c, pl.ds(2 * t + x, 1), 128 * pair : 128 * (pair + 1)] = jnp.where(
                        low_half, a[t, 2 * pair : 2 * pair + 1], b[t, 2 * pair + 1 : 2 * pair + 2])

    spread(0, magnet[...])
    wide[:, :, 0:3, 1] = jnp.zeros((1 + STEPS, 3, 3, LY, 128), jnp.float32)
    wide[:, :, 5:8, 1] = jnp.zeros((1 + STEPS, 3, 3, LY, 128), jnp.float32)

    barrier = pltpu.get_barrier_semaphore()
    diagonal = [(dx, dy) for dx, dy in OFFSETS if dx and dy]
    for i in range(1, nx):
        pl.semaphore_signal(barrier, 1, device_id=(lax.rem(me_x + i, nx), me_y), device_id_type=MESH)
    for i in range(1, ny):
        pl.semaphore_signal(barrier, 1, device_id=(me_x, lax.rem(me_y + i, ny)), device_id_type=MESH)
    for dx, dy in diagonal:
        @pl.when(present(dx, dy))
        def _():
            pl.semaphore_signal(barrier, 1, device_id=(me_x + dx, me_y + dy), device_id_type=MESH)
    beside_x = jnp.minimum(me_x, 2) + jnp.minimum(nx - 1 - me_x, 2)
    beside_y = jnp.minimum(me_y, 1) + jnp.minimum(ny - 1 - me_y, 1)
    pl.semaphore_wait(barrier, nx + ny - 2 + beside_x * beside_y)

    def along_y(i, src, dst, send, recv):
        return pltpu.make_async_remote_copy(
            src, dst, send.at[i], recv.at[i],
            device_id=(me_x, lax.rem(me_y + i, ny)), device_id_type=MESH)

    def along_x(i, src, dst, send, recv):
        return pltpu.make_async_remote_copy(
            src, dst, send.at[i], recv.at[i],
            device_id=(lax.rem(me_x + i, nx), me_y), device_id_type=MESH)

    far_first = sorted(range(1, nx), key=lambda i: abs(2 * i - nx))

    gather = [along_y(i, fields.at[0], rows_in.at[me_y], ag_send, ag_recv) for i in range(1, ny)]
    for copy in gather:
        copy.start()

    def side(i):
        if i < 4:
            d = (-2, -1, 1, 2)[i]
            at, first, count = PLACE[-d]
            many = 2 if abs(d) == 2 else 1 + STEPS
            src = fields.at[pl.ds(0, many), :, pl.ds(first, count)]
            dst = wide.at[pl.ds(0, many), :, pl.ds(at, count), 1]
            return d, 0, src, dst
        d = (-1, 1)[i - 4]
        return 0, d, wide.at[:, :, :, 1], wide.at[:, :, :, 1 - d]

    def side_copy(i):
        dx, dy, src, dst = side(i)
        return pltpu.make_async_remote_copy(
            src, dst, side_send.at[i], side_recv.at[i],
            device_id=(me_x + dx, me_y + dy), device_id_type=MESH)

    def side_start(which):
        for i in which:
            @pl.when(present(*side(i)[:2]))
            def _():
                side_copy(i).start()

    def side_wait(which):
        for i in which:
            dx, dy = side(i)[:2]

            @pl.when(present(dx, dy))
            def _():
                side_copy(i).wait_send()

            @pl.when(present(-dx, -dy))
            def _():
                side_copy(i).wait_recv()

    def halo(i):
        dx, dy = OFFSETS[i]
        at, first, count = PLACE[-dx]
        return pltpu.make_async_remote_copy(
            demag.at[:, pl.ds(first, count)], wide_demag.at[:, pl.ds(at, count), 1 - dy],
            dem_send.at[i], dem_recv.at[i],
            device_id=(me_x + dx, me_y + dy), device_id_type=MESH)

    for s in range(STEPS):
        spread(1 + s, thermal[s])
    side_start(range(4))
    for i in (4, 2, 3, 5):
        loads[i].start()
    wide[0:4, :, 3:5, 1] = fields[...]
    rows_in[me_y] = fields[0]

    loads[1].wait()
    z_fwd[...] = jnp.zeros_like(z_fwd)
    for x in range(2):
        for part in range(6):
            z_fwd[:, pl.ds(128 * part + NZ * x, NZ), 128 * x : 128 * (x + 1)] = z_small[:, pl.ds(NZ * part, NZ)]
    loads[0].wait()
    for copy in gather:
        copy.wait()
    data = jnp.concatenate(
        [rows_in[:, c, t].reshape(y_all, 128) for c in range(3) for t in range(2)], axis=1)
    spectrum = dot_thin(y_fwd, data)
    joined = []
    for t in range(2):
        parts = []
        for c in range(3):
            lanes = slice((2 * c + t) * 128, (2 * c + t + 1) * 128)
            parts += [spectrum[: 2 * y_all, lanes], spectrum[2 * y_all :, lanes]]
        joined.append(jnp.concatenate(parts, axis=1))
    planes = dot_right(jnp.concatenate(joined, axis=0), z_fwd)
    for t in range(2):
        for x in range(2):
            piece = planes[t * 2 * y_all : (t + 1) * 2 * y_all, x * 128 : (x + 1) * 128]
            spec_out[:, 2 * t + x] = piece.reshape(nx, 8, 128)
    forward = [
        along_x(i, spec_out.at[lax.rem(me_x + i, nx)], spec_in.at[me_x], fwd_send, fwd_recv)
        for i in far_first
    ]
    for copy in forward:
        copy.start()
    for i in (6, 7, 8):
        loads[i].start()
    spec_in[me_x] = spec_out[me_x]

    for i in (2, 3, 4):
        loads[i].wait()
    for y in range(8):
        for source, first, last in ((diag, 0, 128), (off, 128, 384)):
            piece = source[:, :, y, :].reshape(3 * block, 2 * x_all)
            high, low = split(piece)
            both = jnp.concatenate([high, low], axis=0)
            tensor[pl.ds(y * 2 * x_all, 2 * x_all), first:last] = lax.dot_general(
                both, place[:, first:last], (((0,), (0,)), ((), ())), preferred_element_type=jnp.float32)
    loads[5].wait()
    for a in range(8):
        own = lax.rem(lax.broadcasted_iota(jnp.int32, (1, 1, 8 * x_all), 2), 8) == a
        own = jnp.where(own, 1.0, 0.0).astype(jnp.bfloat16)
        for part in range(2):
            x_fwd[:, pl.ds((part * 8 + a) * 2 * x_all, 2 * x_all)] = (
                x_small[:, pl.ds(part * 2 * x_all, 2 * x_all)] * own)
    loads[6].wait()
    for copy in forward:
        copy.wait()
    side_wait(range(4))
    side_start((4, 5))

    size = 8 * 2 * x_all
    both = dot_left(x_fwd, spec_in[...].reshape(x_all * 8, 128))
    spectra = both[:size] + turn * pltpu.roll(both[size:], 64, 1)
    second = jnp.where(component < 2 * kept, pltpu.roll(spectra, 128 - kept, 1), pltpu.roll(spectra, 2 * kept, 1))
    third = jnp.where(component < kept, pltpu.roll(spectra, 128 - 2 * kept, 1), pltpu.roll(spectra, kept, 1))
    response = tensor[:, :128] * spectra + tensor[:, 128:256] * second + tensor[:, 256:] * third
    both = dot_left(x_inv, response)
    back = both[: x_all * 8] - turn * pltpu.roll(both[x_all * 8 :], 64, 1)
    back_out[...] = back.reshape(nx, LX, 8, 128)
    inverse = [
        along_x(i, back_out.at[lax.rem(me_x + i, nx)], back_in.at[me_x], inv_send, inv_recv)
        for i in far_first
    ]
    for copy in inverse:
        copy.start()
    back_in[me_x] = back_out[me_x]
    loads[7].wait()
    loads[8].wait()
    for copy in inverse:
        copy.wait()
    data = jnp.concatenate([back_in[:, x].reshape(nx * 8, 128) for x in range(LX)], axis=1)
    both = dot_thin(y_inv, data)
    for x in range(LX):
        lanes = slice(x * 128, (x + 1) * 128)
        rows = both[:y_all, lanes] - turn * pltpu.roll(both[y_all:, lanes], 64, 1)
        row_out[:, x] = rows.reshape(ny, LY, 128)
    final = [
        along_y(i, row_out.at[lax.rem(me_y + i, ny)], row_in.at[me_y], last_send, last_recv)
        for i in range(1, ny)
    ]
    for copy in final:
        copy.start()
    row_in[me_y] = row_out[me_y]
    for copy in final:
        copy.wait()
    data = jnp.concatenate([row_in[g].reshape(LX * LY, 128) for g in range(ny)], axis=1)
    rows = dot_right(data, z_inv)
    turned = jnp.concatenate(
        [pltpu.roll(rows[:, :128], 64, 1), pltpu.roll(rows[:, 128:], 64, 1)], axis=1)
    for c, (a, b, first) in enumerate(((rows, turned, 0), (turned, rows, 0), (rows, turned, 128))):
        a, b = a[:, first : first + 128], b[:, first : first + 128]
        for t in range(2):
            demag[c, t] = jnp.where(low_half, a[16 * t : 16 * t + 8], b[16 * t + 8 : 16 * t + 16])
    for i, (dx, dy) in enumerate(OFFSETS):
        @pl.when(present(dx, dy))
        def _():
            halo(i).start()
    wide_demag[:, 3:5, 1] = demag[...]
    for c in range(3):
        collapse(demag_ref, c, demag[c])
    side_wait((4, 5))
    for i, (dx, dy) in enumerate(OFFSETS):
        @pl.when(present(dx, dy))
        def _():
            halo(i).wait_send()

        @pl.when(present(-dx, -dy))
        def _():
            halo(i).wait_recv()

    shape = (8, 3 * LY, 128)
    lanes = lax.broadcasted_iota(jnp.int32, shape, 2)
    x_at = LX * me_x - 6 + 2 * lax.broadcasted_iota(jnp.int32, shape, 0) + lanes // 64
    y_at = LY * me_y - LY + lax.broadcasted_iota(jnp.int32, shape, 1)
    z_at = lax.rem(lanes, 64)
    left_half = lanes < 64
    at_x0, at_x1 = x_at == 0, x_at == x_all - 1
    at_y0, at_y1 = y_at == 0, y_at == y_all - 1
    at_z0, at_z1 = z_at == 0, z_at == NZ - 1

    def laplace(v):
        turned = pltpu.roll(v, 64, 2)
        up = jnp.where(left_half, turned, jnp.concatenate([turned[1:], turned[-1:]], axis=0))
        down = jnp.where(left_half, jnp.concatenate([turned[:1], turned[:-1]], axis=0), turned)
        total = jnp.where(at_x1, v, up) + jnp.where(at_x0, v, down)
        total = total + jnp.where(at_y1, v, pltpu.roll(v, 3 * LY - 1, 1))
        total = total + jnp.where(at_y0, v, pltpu.roll(v, 1, 1))
        total = total + jnp.where(at_z1, v, pltpu.roll(v, 127, 2))
        total = total + jnp.where(at_z0, v, pltpu.roll(v, 1, 2))
        return total - 6.0 * v

    def torque(v, noise):
        h = [laplace(v[c]) + noise[c] for c in range(3)]
        h[2] = h[2] + ANISOTROPY * v[2]
        first = cross(v, h)
        second = cross(v, first)
        return [(first[c] + DAMPING * second[c]) * (-1.0 / (1.0 + DAMPING * DAMPING)) for c in range(3)]

    m = [wide[0, c].reshape(shape) for c in range(3)]
    for s in range(STEPS):
        noise = [wide_demag[c].reshape(shape) + wide[1 + s, c].reshape(shape) for c in range(3)]
        f0 = torque(m, noise)
        f1 = torque([m[c] + TIME_STEP * f0[c] for c in range(3)], noise)
        u = [m[c] + 0.5 * TIME_STEP * (f0[c] + f1[c]) for c in range(3)]
        norm = jnp.sqrt(u[0] * u[0] + u[1] * u[1] + u[2] * u[2])
        m = [u[c] / norm for c in range(3)]
    for c in range(3):
        collapse(final_ref, c, m[c][3:5, LY : 2 * LY])


def body(nx, ny, magnet, thermal, kernel_diag, kernel_off):
    block = 2 * NZ // ny
    x_all, y_all = nx * LX, ny * LY
    consts = tables(nx, ny)
    vmem = pl.BlockSpec(memory_space=pltpu.VMEM)
    anyspace = pl.BlockSpec(memory_space=pl.ANY)
    out = jax.ShapeDtypeStruct(magnet.shape, jnp.float32)
    f32, bf16 = jnp.float32, jnp.bfloat16
    scratch = [
        pltpu.VMEM((1 + STEPS, 3, LX // 2, LY, 128), f32),
        pltpu.VMEM((3, LX // 2, LY, 128), f32),
        pltpu.VMEM(kernel_diag.shape, f32),
        pltpu.VMEM(kernel_off.shape, f32),
        pltpu.VMEM(consts[0].shape, bf16),
        pltpu.VMEM(consts[1].shape[1:], bf16),
        pltpu.VMEM((2, 3 * 2 * 2 * NZ, 256), bf16),
        pltpu.VMEM(consts[2].shape, bf16),
        pltpu.VMEM((2, 2 * 8 * 2 * x_all, 8 * x_all), bf16),
        *[pltpu.VMEM(c.shape, bf16) for c in consts[3:]],
        pltpu.VMEM((1 + STEPS, 3, 8, 3, LY, 128), f32),
        pltpu.VMEM((3, 8, 3, LY, 128), f32),
        pltpu.VMEM((ny, 3, 2, LY, 128), f32),
        *[pltpu.VMEM((nx, LX, 8, 128), f32)] * 4,
        *[pltpu.VMEM((ny, LX, LY, 128), f32)] * 2,
        pltpu.VMEM((8 * 2 * x_all, 384), f32),
        pltpu.SemaphoreType.DMA((9,)),
        *[pltpu.SemaphoreType.DMA((6,))] * 2,
        *[pltpu.SemaphoreType.DMA((len(OFFSETS),))] * 2,
        *[pltpu.SemaphoreType.DMA((ny,))] * 2,
        *[pltpu.SemaphoreType.DMA((nx,))] * 4,
        *[pltpu.SemaphoreType.DMA((ny,))] * 2,
    ]
    return pl.pallas_call(
        functools.partial(kernel, nx, ny),
        out_shape=(out, out),
        in_specs=[vmem, vmem] + [anyspace] * 9,
        out_specs=(vmem, vmem),
        scratch_shapes=scratch,
        compiler_params=pltpu.CompilerParams(
            collective_id=0, has_side_effects=True, vmem_limit_bytes=56 * 1024 * 1024),
    )(magnet, thermal, kernel_diag, kernel_off, *[jnp.asarray(c) for c in consts])


def solution(mesh):
    in_specs = (
        P(None, "gx", "gy"),
        P(None, None, "gx", "gy"),
        P(None, "gy", "gx", None),
        P(None, "gy", "gx", None),
    )
    out_specs = (P(None, "gx", "gy"), P(None, "gx", "gy"))
    run = functools.partial(body, mesh.shape["gx"], mesh.shape["gy"])
    return jax.shard_map(run, mesh=mesh, in_specs=in_specs, out_specs=out_specs, check_vma=False)
```

```python
import functools

import jax
import jax.numpy as jnp
import ml_dtypes
import numpy as np
from jax import lax
from jax.experimental import pallas as pl
from jax.experimental.pallas import tpu as pltpu
from jax.sharding import PartitionSpec as P

NZ = 64
STEPS = 3
DAMPING = 0.1
TIME_STEP = 0.05
ANISOTROPY = 0.5
LX = 4
LY = 8
MESH = pl.DeviceIdType.MESH
OFFSETS = [(dx, dy) for dx in (-2, -1, 0, 1, 2) for dy in (-1, 0, 1) if (dx, dy) != (0, 0)]
PLACE = {-2: (0, 1, 1), -1: (1, 0, 2), 0: (3, 0, 2), 1: (5, 0, 2), 2: (7, 0, 1)}


def halves(table):
    table = np.asarray(table, np.float32)
    high = table.astype(ml_dtypes.bfloat16)
    low = (table - high.astype(np.float32)).astype(ml_dtypes.bfloat16)
    return np.stack([high, low])


def beside(table):
    high, low = halves(table)
    return np.concatenate([high, low, high], axis=1)


def angles(first, second, period):
    return 2.0 * np.pi * ((np.asarray(first)[:, None] * np.asarray(second)[None, :]) % period) / period


def tables(nx, ny):
    x_all, y_all = nx * LX, ny * LY
    block = 2 * NZ // ny
    kept = block // 2 + 1
    ang = angles(np.arange(2 * y_all), np.arange(y_all), 2 * y_all)
    y_fwd = np.concatenate([np.cos(ang), -np.sin(ang)])
    z_fwd = np.zeros((ny, 3, 2, NZ, 128))
    z_inv = np.zeros((ny, 128, 4, NZ))
    for g in range(ny):
        kz = g * block + np.arange(kept)
        ang = angles(np.arange(NZ), kz, 2 * NZ)
        weight = np.full((kept,), 2.0)
        if g in (0, ny // 2):
            weight[0] = 1.0
        if g > ny // 2:
            weight[0] = 0.0
        if g < ny // 2:
            weight[kept - 1] = 0.0
        weight = -weight / (8.0 * x_all * y_all * NZ)
        for c in range(3):
            re = slice(c * kept, (c + 1) * kept)
            im = slice(64 + c * kept, 64 + (c + 1) * kept)
            z_fwd[g, c, 0, :, re] = np.cos(ang)
            z_fwd[g, c, 1, :, re] = np.sin(ang)
            z_fwd[g, c, 1, :, im] = np.cos(ang)
            z_fwd[g, c, 0, :, im] = -np.sin(ang)
            z_inv[g, re, c] = (np.cos(ang) * weight).T
            z_inv[g, im, c] = (-np.sin(ang) * weight).T
    z_fwd = z_fwd.reshape(ny, 3 * 2 * NZ, 128)
    z_inv = z_inv.reshape(ny * 128, 4 * NZ)
    ang = angles(np.arange(2 * x_all), np.arange(x_all), 2 * x_all)
    eye = np.eye(8)
    x_fwd = np.stack([np.cos(ang), np.sin(ang)])
    x_inv = np.einsum("skx,ab->sxabk", x_fwd, eye).reshape(2 * x_all * 8, 8 * 2 * x_all)
    x_fwd = np.repeat(x_fwd.reshape(2 * 2 * x_all, x_all), 8, axis=1)
    ang = angles(np.arange(y_all), np.arange(2 * y_all), 2 * y_all)
    y_inv = np.concatenate([np.cos(ang), np.sin(ang)])
    place = np.zeros((3, 2, 3, block, 128))
    pairs = {(0, 1): 0, (0, 2): 1, (1, 2): 2}
    for c in range(3):
        for d in range(3):
            other = (c + d) % 3
            entry = c if d == 0 else pairs[(min(c, other), max(c, other))]
            for half in range(2):
                for j in range(kept):
                    place[d, :, entry, j, half * 64 + c * kept + j] = 1.0
    place = place.reshape(3, 6 * block, 128)
    place = np.concatenate([place[0], place[1], place[2]], axis=1).astype(ml_dtypes.bfloat16)
    return (
        beside(y_fwd),
        np.moveaxis(halves(z_fwd), 0, 1),
        halves(x_fwd),
        halves(x_inv),
        beside(y_inv),
        halves(z_inv),
        place,
    )


def split(value):
    high = value.astype(jnp.bfloat16)
    low = (value - high.astype(jnp.float32)).astype(jnp.bfloat16)
    return high, low


def dot(left, right):
    return jnp.dot(left, right, preferred_element_type=jnp.float32)


def dot_left(table, data):
    high, low = split(data)
    both = dot(table[0], jnp.concatenate([high, low], axis=1))
    lanes = data.shape[1]
    return both[:, :lanes] + (both[:, lanes:] + dot(table[1], high))


def dot_thin(table, data):
    high, low = split(data)
    return dot(table[...], jnp.concatenate([high, high, low], axis=0))


def dot_right(data, table):
    high, low = split(data)
    both = dot(jnp.concatenate([high, low], axis=0), table[0])
    rows = data.shape[0]
    return both[:rows] + (both[rows:] + dot(high, table[1]))


def cross(a, b):
    return [a[1] * b[2] - a[2] * b[1], a[2] * b[0] - a[0] * b[2], a[0] * b[1] - a[1] * b[0]]


def kernel(
    nx, ny,
    magnet, thermal, diag_h, off_h, y_fwd_h, z_fwd_h, x_fwd_h, x_inv_h, y_inv_h, z_inv_h, place_h,
    final_ref, demag_ref,
    fields, demag, diag, off, y_fwd, z_small, z_fwd, x_small, x_fwd, x_inv, y_inv, z_inv, place,
    wide, wide_demag, rows_in, spec_out, spec_in, back_out, back_in, row_out, row_in, tensor,
    local_sem, side_send, side_recv, dem_send, dem_recv, ag_send, ag_recv,
    fwd_send, fwd_recv, inv_send, inv_recv, last_send, last_recv,
):
    x_all, y_all = nx * LX, ny * LY
    block = 2 * NZ // ny
    kept = block // 2 + 1
    me_x, me_y = lax.axis_index("gx"), lax.axis_index("gy")

    loads = [
        pltpu.make_async_copy(src, dst, local_sem.at[i])
        for i, (src, dst) in enumerate([
            (y_fwd_h, y_fwd), (z_fwd_h.at[me_y], z_small), (diag_h, diag), (off_h, off),
            (place_h, place), (x_fwd_h, x_small), (x_inv_h, x_inv), (y_inv_h, y_inv), (z_inv_h, z_inv),
        ])
    ]
    for i in (1, 0):
        loads[i].start()

    def present(dx, dy):
        x, y = me_x + dx, me_y + dy
        return (x >= 0) & (x < nx) & (y >= 0) & (y < ny)

    lane = lax.broadcasted_iota(jnp.int32, (1, 128), 1)
    low_half = lane < 64
    component = lax.rem(lane, 64)
    turn = jnp.where(low_half, 1.0, -1.0).astype(jnp.float32)

    def spread(to, value):
        for pair in range(LY // 2):
            same = value[:, :, 128 * pair : 128 * (pair + 1)]
            other = pltpu.roll(same, 64, 2)
            for t in range(LX // 2):
                for y in range(2):
                    a, b = (same, other) if y == 0 else (other, same)
                    fields[to, :, t, pl.ds(2 * pair + y, 1)] = jnp.where(
                        low_half[None], a[:, 2 * t : 2 * t + 1], b[:, 2 * t + 1 : 2 * t + 2])

    def collapse(ref, c, same):
        other = pltpu.roll(same, 64, 2)
        for t in range(LX // 2):
            for x in range(2):
                a, b = (same, other) if x == 0 else (other, same)
                for pair in range(LY // 2):
                    ref[c, pl.ds(2 * t + x, 1), 128 * pair : 128 * (pair + 1)] = jnp.where(
                        low_half, a[t, 2 * pair : 2 * pair + 1], b[t, 2 * pair + 1 : 2 * pair + 2])

    wide[:, :, 0:3, 1] = jnp.zeros((1 + STEPS, 3, 3, LY, 128), jnp.float32)
    wide[:, :, 5:8, 1] = jnp.zeros((1 + STEPS, 3, 3, LY, 128), jnp.float32)

    barrier = pltpu.get_barrier_semaphore()
    diagonal = [(dx, dy) for dx, dy in OFFSETS if dx and dy]
    for i in range(1, nx):
        pl.semaphore_signal(barrier, 1, device_id=(lax.rem(me_x + i, nx), me_y), device_id_type=MESH)
    for i in range(1, ny):
        pl.semaphore_signal(barrier, 1, device_id=(me_x, lax.rem(me_y + i, ny)), device_id_type=MESH)
    for dx, dy in diagonal:
        @pl.when(present(dx, dy))
        def _():
            pl.semaphore_signal(barrier, 1, device_id=(me_x + dx, me_y + dy), device_id_type=MESH)
    beside_x = jnp.minimum(me_x, 2) + jnp.minimum(nx - 1 - me_x, 2)
    beside_y = jnp.minimum(me_y, 1) + jnp.minimum(ny - 1 - me_y, 1)
    spread(0, magnet[...])
    for s in range(STEPS):
        spread(1 + s, thermal[s])
    pl.semaphore_wait(barrier, nx + ny - 2 + beside_x * beside_y)

    def along_y(i, src, dst, send, recv):
        return pltpu.make_async_remote_copy(
            src, dst, send.at[i], recv.at[i],
            device_id=(me_x, lax.rem(me_y + i, ny)), device_id_type=MESH)

    def along_x(i, src, dst, send, recv):
        return pltpu.make_async_remote_copy(
            src, dst, send.at[i], recv.at[i],
            device_id=(lax.rem(me_x + i, nx), me_y), device_id_type=MESH)

    far_first = sorted(range(1, nx), key=lambda i: abs(2 * i - nx))

    gather = [along_y(i, fields.at[0], rows_in.at[me_y], ag_send, ag_recv) for i in range(1, ny)]
    for copy in gather:
        copy.start()

    def side(i):
        if i < 4:
            d = (-2, -1, 1, 2)[i]
            at, first, count = PLACE[-d]
            many = 2 if abs(d) == 2 else 1 + STEPS
            src = fields.at[pl.ds(0, many), :, pl.ds(first, count)]
            dst = wide.at[pl.ds(0, many), :, pl.ds(at, count), 1]
            return d, 0, src, dst
        d = (-1, 1)[i - 4]
        return 0, d, wide.at[:, :, :, 1], wide.at[:, :, :, 1 - d]

    def side_copy(i):
        dx, dy, src, dst = side(i)
        return pltpu.make_async_remote_copy(
            src, dst, side_send.at[i], side_recv.at[i],
            device_id=(me_x + dx, me_y + dy), device_id_type=MESH)

    def side_start(which):
        for i in which:
            @pl.when(present(*side(i)[:2]))
            def _():
                side_copy(i).start()

    def side_wait(which):
        for i in which:
            dx, dy = side(i)[:2]

            @pl.when(present(dx, dy))
            def _():
                side_copy(i).wait_send()

            @pl.when(present(-dx, -dy))
            def _():
                side_copy(i).wait_recv()

    def halo(i):
        dx, dy = OFFSETS[i]
        at, first, count = PLACE[-dx]
        return pltpu.make_async_remote_copy(
            demag.at[:, pl.ds(first, count)], wide_demag.at[:, pl.ds(at, count), 1 - dy],
            dem_send.at[i], dem_recv.at[i],
            device_id=(me_x + dx, me_y + dy), device_id_type=MESH)

    side_start(range(4))
    for i in (4, 2, 3, 5):
        loads[i].start()
    wide[0:4, :, 3:5, 1] = fields[...]
    rows_in[me_y] = fields[0]

    loads[1].wait()
    z_fwd[...] = jnp.zeros_like(z_fwd)
    for x in range(2):
        for part in range(6):
            z_fwd[:, pl.ds(128 * part + NZ * x, NZ), 128 * x : 128 * (x + 1)] = z_small[:, pl.ds(NZ * part, NZ)]
    loads[0].wait()
    for copy in gather:
        copy.wait()
    data = jnp.concatenate(
        [rows_in[:, c, t].reshape(y_all, 128) for c in range(3) for t in range(2)], axis=1)
    spectrum = dot_thin(y_fwd, data)
    joined = []
    for t in range(2):
        parts = []
        for c in range(3):
            lanes = slice((2 * c + t) * 128, (2 * c + t + 1) * 128)
            parts += [spectrum[: 2 * y_all, lanes], spectrum[2 * y_all :, lanes]]
        joined.append(jnp.concatenate(parts, axis=1))
    planes = dot_right(jnp.concatenate(joined, axis=0), z_fwd)
    for t in range(2):
        for x in range(2):
            piece = planes[t * 2 * y_all : (t + 1) * 2 * y_all, x * 128 : (x + 1) * 128]
            spec_out[:, 2 * t + x] = piece.reshape(nx, 8, 128)
    forward = [
        along_x(i, spec_out.at[lax.rem(me_x + i, nx)], spec_in.at[me_x], fwd_send, fwd_recv)
        for i in far_first
    ]
    for copy in forward:
        copy.start()
    for i in (6, 7, 8):
        loads[i].start()
    spec_in[me_x] = spec_out[me_x]

    for i in (2, 3, 4):
        loads[i].wait()
    for y in range(8):
        for source, first, last in ((diag, 0, 128), (off, 128, 384)):
            piece = source[:, :, y, :].reshape(3 * block, 2 * x_all)
            high, low = split(piece)
            both = jnp.concatenate([high, low], axis=0)
            tensor[pl.ds(y * 2 * x_all, 2 * x_all), first:last] = lax.dot_general(
                both, place[:, first:last], (((0,), (0,)), ((), ())), preferred_element_type=jnp.float32)
    loads[5].wait()
    for a in range(8):
        own = lax.rem(lax.broadcasted_iota(jnp.int32, (1, 1, 8 * x_all), 2), 8) == a
        own = jnp.where(own, 1.0, 0.0).astype(jnp.bfloat16)
        for part in range(2):
            x_fwd[:, pl.ds((part * 8 + a) * 2 * x_all, 2 * x_all)] = (
                x_small[:, pl.ds(part * 2 * x_all, 2 * x_all)] * own)
    loads[6].wait()
    for copy in forward:
        copy.wait()
    side_wait(range(4))
    side_start((4, 5))

    size = 8 * 2 * x_all
    both = dot_left(x_fwd, spec_in[...].reshape(x_all * 8, 128))
    spectra = both[:size] + turn * pltpu.roll(both[size:], 64, 1)
    second = jnp.where(component < 2 * kept, pltpu.roll(spectra, 128 - kept, 1), pltpu.roll(spectra, 2 * kept, 1))
    third = jnp.where(component < kept, pltpu.roll(spectra, 128 - 2 * kept, 1), pltpu.roll(spectra, kept, 1))
    response = tensor[:, :128] * spectra + tensor[:, 128:256] * second + tensor[:, 256:] * third
    both = dot_left(x_inv, response)
    back = both[: x_all * 8] - turn * pltpu.roll(both[x_all * 8 :], 64, 1)
    back_out[...] = back.reshape(nx, LX, 8, 128)
    inverse = [
        along_x(i, back_out.at[lax.rem(me_x + i, nx)], back_in.at[me_x], inv_send, inv_recv)
        for i in far_first
    ]
    for copy in inverse:
        copy.start()
    back_in[me_x] = back_out[me_x]
    loads[7].wait()
    loads[8].wait()
    for copy in inverse:
        copy.wait()
    data = jnp.concatenate([back_in[:, x].reshape(nx * 8, 128) for x in range(LX)], axis=1)
    both = dot_thin(y_inv, data)
    for x in range(LX):
        lanes = slice(x * 128, (x + 1) * 128)
        rows = both[:y_all, lanes] - turn * pltpu.roll(both[y_all:, lanes], 64, 1)
        row_out[:, x] = rows.reshape(ny, LY, 128)
    final = [
        along_y(i, row_out.at[lax.rem(me_y + i, ny)], row_in.at[me_y], last_send, last_recv)
        for i in range(1, ny)
    ]
    for copy in final:
        copy.start()
    row_in[me_y] = row_out[me_y]
    for copy in final:
        copy.wait()
    data = jnp.concatenate([row_in[g].reshape(LX * LY, 128) for g in range(ny)], axis=1)
    rows = dot_right(data, z_inv)
    turned = jnp.concatenate(
        [pltpu.roll(rows[:, :128], 64, 1), pltpu.roll(rows[:, 128:], 64, 1)], axis=1)
    for c, (a, b, first) in enumerate(((rows, turned, 0), (turned, rows, 0), (rows, turned, 128))):
        a, b = a[:, first : first + 128], b[:, first : first + 128]
        for t in range(2):
            demag[c, t] = jnp.where(low_half, a[16 * t : 16 * t + 8], b[16 * t + 8 : 16 * t + 16])
    for i, (dx, dy) in enumerate(OFFSETS):
        @pl.when(present(dx, dy))
        def _():
            halo(i).start()
    wide_demag[:, 3:5, 1] = demag[...]
    for c in range(3):
        collapse(demag_ref, c, demag[c])
    side_wait((4, 5))
    for i, (dx, dy) in enumerate(OFFSETS):
        @pl.when(present(dx, dy))
        def _():
            halo(i).wait_send()

        @pl.when(present(-dx, -dy))
        def _():
            halo(i).wait_recv()

    shape = (8, 3 * LY, 128)
    lanes = lax.broadcasted_iota(jnp.int32, shape, 2)
    x_at = LX * me_x - 6 + 2 * lax.broadcasted_iota(jnp.int32, shape, 0) + lanes // 64
    y_at = LY * me_y - LY + lax.broadcasted_iota(jnp.int32, shape, 1)
    z_at = lax.rem(lanes, 64)
    left_half = lanes < 64
    at_x0, at_x1 = x_at == 0, x_at == x_all - 1
    at_y0, at_y1 = y_at == 0, y_at == y_all - 1
    at_z0, at_z1 = z_at == 0, z_at == NZ - 1

    def laplace(v):
        turned = pltpu.roll(v, 64, 2)
        up = jnp.where(left_half, turned, jnp.concatenate([turned[1:], turned[-1:]], axis=0))
        down = jnp.where(left_half, jnp.concatenate([turned[:1], turned[:-1]], axis=0), turned)
        total = jnp.where(at_x1, v, up) + jnp.where(at_x0, v, down)
        total = total + jnp.where(at_y1, v, pltpu.roll(v, 3 * LY - 1, 1))
        total = total + jnp.where(at_y0, v, pltpu.roll(v, 1, 1))
        total = total + jnp.where(at_z1, v, pltpu.roll(v, 127, 2))
        total = total + jnp.where(at_z0, v, pltpu.roll(v, 1, 2))
        return total - 6.0 * v

    def torque(v, noise):
        h = [laplace(v[c]) + noise[c] for c in range(3)]
        h[2] = h[2] + ANISOTROPY * v[2]
        first = cross(v, h)
        second = cross(v, first)
        return [(first[c] + DAMPING * second[c]) * (-1.0 / (1.0 + DAMPING * DAMPING)) for c in range(3)]

    m = [wide[0, c].reshape(shape) for c in range(3)]
    for s in range(STEPS):
        noise = [wide_demag[c].reshape(shape) + wide[1 + s, c].reshape(shape) for c in range(3)]
        f0 = torque(m, noise)
        f1 = torque([m[c] + TIME_STEP * f0[c] for c in range(3)], noise)
        u = [m[c] + 0.5 * TIME_STEP * (f0[c] + f1[c]) for c in range(3)]
        norm = jnp.sqrt(u[0] * u[0] + u[1] * u[1] + u[2] * u[2])
        m = [u[c] / norm for c in range(3)]
    for c in range(3):
        collapse(final_ref, c, m[c][3:5, LY : 2 * LY])


def body(nx, ny, magnet, thermal, kernel_diag, kernel_off):
    block = 2 * NZ // ny
    x_all, y_all = nx * LX, ny * LY
    consts = tables(nx, ny)
    vmem = pl.BlockSpec(memory_space=pltpu.VMEM)
    anyspace = pl.BlockSpec(memory_space=pl.ANY)
    out = jax.ShapeDtypeStruct(magnet.shape, jnp.float32)
    f32, bf16 = jnp.float32, jnp.bfloat16
    scratch = [
        pltpu.VMEM((1 + STEPS, 3, LX // 2, LY, 128), f32),
        pltpu.VMEM((3, LX // 2, LY, 128), f32),
        pltpu.VMEM(kernel_diag.shape, f32),
        pltpu.VMEM(kernel_off.shape, f32),
        pltpu.VMEM(consts[0].shape, bf16),
        pltpu.VMEM(consts[1].shape[1:], bf16),
        pltpu.VMEM((2, 3 * 2 * 2 * NZ, 256), bf16),
        pltpu.VMEM(consts[2].shape, bf16),
        pltpu.VMEM((2, 2 * 8 * 2 * x_all, 8 * x_all), bf16),
        *[pltpu.VMEM(c.shape, bf16) for c in consts[3:]],
        pltpu.VMEM((1 + STEPS, 3, 8, 3, LY, 128), f32),
        pltpu.VMEM((3, 8, 3, LY, 128), f32),
        pltpu.VMEM((ny, 3, 2, LY, 128), f32),
        *[pltpu.VMEM((nx, LX, 8, 128), f32)] * 4,
        *[pltpu.VMEM((ny, LX, LY, 128), f32)] * 2,
        pltpu.VMEM((8 * 2 * x_all, 384), f32),
        pltpu.SemaphoreType.DMA((9,)),
        *[pltpu.SemaphoreType.DMA((6,))] * 2,
        *[pltpu.SemaphoreType.DMA((len(OFFSETS),))] * 2,
        *[pltpu.SemaphoreType.DMA((ny,))] * 2,
        *[pltpu.SemaphoreType.DMA((nx,))] * 4,
        *[pltpu.SemaphoreType.DMA((ny,))] * 2,
    ]
    return pl.pallas_call(
        functools.partial(kernel, nx, ny),
        out_shape=(out, out),
        in_specs=[vmem, vmem] + [anyspace] * 9,
        out_specs=(vmem, vmem),
        scratch_shapes=scratch,
        compiler_params=pltpu.CompilerParams(
            collective_id=0, has_side_effects=True, vmem_limit_bytes=56 * 1024 * 1024),
    )(magnet, thermal, kernel_diag, kernel_off, *[jnp.asarray(c) for c in consts])


def solution(mesh):
    in_specs = (
        P(None, "gx", "gy"),
        P(None, None, "gx", "gy"),
        P(None, "gy", "gx", None),
        P(None, "gy", "gx", None),
    )
    out_specs = (P(None, "gx", "gy"), P(None, "gx", "gy"))
    run = functools.partial(body, mesh.shape["gx"], mesh.shape["gy"])
    return jax.shard_map(run, mesh=mesh, in_specs=in_specs, out_specs=out_specs, check_vma=False)
```
